32 devices in a mesh: groups: 2 (over x), col: 16 (over z, y, core).
Axes of the slice: x: 2, y: 2, z: 4, core: 2. Of those that a mesh axis runs over, the one named last changes fastest.
Arguments:
- features: bfloat16 [32, 8, 8192], P(('groups', 'col')), parts along dimension 0
- zone_ids: int32 [32], P(('groups', 'col')), parts along dimension 0, may hold values from 0 to 7, as said below
- golden_owner: int32 [16], P('groups'), parts along dimension 0, may hold values from 0 to 15, as said below
- defect_mask: int32 [32, 8, 128], P(('groups', 'col')), parts along dimension 0, may hold values 0 or 1
- kernels: bfloat16 [2, 576, 64], replicated, may hold values from -0.25 to 0.25
Outputs:
- score: float32 [32, 8, 128], P(('groups', 'col')), parts along dimension 0
The draws below stay inside these ranges and needn't reach their ends.
There are 2 independent parts, one for each index of `groups`. The reference program is written for one: setup_inputs(seed, part) draws one part's arguments, and reference() takes and returns one part's arrays. A program takes and returns all parts, laid end to end along the dimension named above; an argument that names none is the same for every part. Nothing has to cross between parts.
Inputs may be any that keep to these rules, and one draw needn't show every extreme that they name: `zone_ids`: every zone holds at least one die. golden_owner[z] is a die of zone z.
All inputs are finite; a program needn't handle non-finite values. No bound on the sum of `defect_mask` on one device may be relied on, other than what follows from the above.
Results may differ from the reference program's by a relative error of at most 0.0039.
Values may be sent and summed in bfloat16 or wider, within the bound.
A program may use at most 64 MiB of HBM per device.

```python
import jax
import jax.numpy as jnp
from jax import lax

C = 64
H = 8
W = 128
SHIFT = 6
BOX = 5
Z = 8
DIES = 16


def layout(key):
    base = jax.random.fold_in(key, 101)
    key_order = jax.random.fold_in(base, 1)
    key_map = jax.random.fold_in(base, 2)
    key_pick = jax.random.fold_in(base, 3)
    order = jax.random.permutation(key_order, DIES).astype(jnp.int32)
    zone_map = jax.random.permutation(key_map, Z).astype(jnp.int32)
    picks = jax.random.randint(key_pick, (3, DIES), 0, Z)
    common = zone_map[jnp.min(picks, axis=0)]
    slots = jnp.arange(DIES, dtype=jnp.int32)
    assign = jnp.where(slots < Z, slots, common).astype(jnp.int32)
    zones = jnp.zeros((DIES,), jnp.int32).at[order].set(assign)
    owners = order[0:Z]
    return (zones, owners)


def draw_zone_ids(key, part):
    zones, owners = layout(key)
    return zones


def draw_golden_owner(key, part):
    zones, owners = layout(key)
    return owners


def draw_features(key, part):
    zones, owners = layout(key)
    base = jax.random.fold_in(key, 202)
    key_rough = jax.random.fold_in(base, 1)
    key_noise = jax.random.fold_in(base, 2)
    key_rank = jax.random.fold_in(base, 3)
    key_spot = jax.random.fold_in(base, 4)
    key_size = jax.random.fold_in(base, 5)
    key_sign = jax.random.fold_in(base, 7)
    key_magn = jax.random.fold_in(base, 8)
    side = 2 * SHIFT + 1
    others = min(side, 2 * H - 1) * min(side, 2 * W - 1) - 1
    rank = jax.random.permutation(key_rank, Z).astype(jnp.float32)
    share = 0.24 + 0.09 * rank / (Z - 1)
    rough_scale = jnp.sqrt(share / (1.0 - share))
    leak = 1.2 * others * jnp.exp(-32.0 * share)
    amplify = 1.0 / (leak * rough_scale)
    signs = jnp.where(jax.random.bernoulli(key_sign, 0.5, (Z, C)), 1.0, -1.0).astype(jnp.float32)
    magnitude = jax.random.uniform(key_magn, (Z, C), jnp.float32, 0.8, 1.2)
    rough = jax.random.normal(key_rough, (Z, H, W, C), jnp.float32)
    noise = jax.random.normal(key_noise, (DIES, H, W, C), jnp.float32)
    zone_scale = jnp.ones((Z,), jnp.float32)
    pattern = (signs * magnitude)[:, None, None, :] + rough_scale[:, None, None, None] * rough
    pattern = pattern * amplify[:, None, None, None]
    tiles = jnp.take(pattern, zones, axis=0)
    spots = (jax.random.uniform(key_spot, (DIES, H, W, 1)) < 0.02).astype(jnp.float32)
    spots = 4.0 * spots * jax.random.normal(key_size, (DIES, H, W, C), jnp.float32)
    whole = (tiles + noise + spots) * jnp.take(zone_scale, zones)[:, None, None, None]
    return whole.reshape(DIES, H, W * C).astype(jnp.bfloat16)


def with_ends(values, stream_key, smallest, high):
    spot = [jax.random.randint(jax.random.fold_in(stream_key, axis), (), 0, length) for axis, length in enumerate(values.shape)]
    widest = values.shape.index(max(values.shape))
    next_to = spot[:widest] + [(spot[widest] + 1) % values.shape[widest]] + spot[widest + 1:]
    return values.at[tuple(spot)].set(smallest).at[tuple(next_to)].set(high)


def scatter_about(key, shape, deviation, limit, kind=jnp.bfloat16):
    return jnp.clip(deviation * jax.random.normal(key, shape, jnp.float32), -limit, limit).astype(kind)


def setup_inputs(seed: int = 0, part: int = 0) -> dict:
    keys = jax.random.split(jax.random.key(seed), 6)
    part_splits = jax.random.split(jax.random.fold_in(keys[5], part), 6)
    return {
        "features": draw_features(jax.random.fold_in(jax.random.fold_in(keys[5], part), 71), part),
        "zone_ids": draw_zone_ids(jax.random.fold_in(jax.random.fold_in(keys[5], part), 71), part),
        "golden_owner": draw_golden_owner(jax.random.fold_in(jax.random.fold_in(keys[5], part), 71), part),
        "defect_mask": with_ends((jax.random.randint(part_splits[3], (DIES, H, W), 0, 2) < 1).astype(jnp.int32), jax.random.fold_in(part_splits[3], 1), 0, 1),
        "kernels": scatter_about(keys[4], (2, 9 * C, C), (9 * C) ** -0.5, 0.25),
    }


def box_sum(plane):
    rows = plane.shape[0]
    cols = plane.shape[1]
    reach = BOX // 2
    padded = jnp.pad(plane, ((reach, reach), (reach, reach)))
    across = padded[0:rows]
    for offset in range(1, BOX):
        across = across + padded[offset:offset + rows]
    total = across[:, 0:cols]
    for offset in range(1, BOX):
        total = total + across[:, offset:offset + cols]
    return total

def align_golden(test_tile, golden_tile):
    height, width, chans = test_tile.shape
    side = 2 * SHIFT + 1
    test_f = test_tile.astype(jnp.float32)
    padded = jnp.pad(golden_tile.astype(jnp.float32), ((SHIFT, SHIFT), (SHIFT, SHIFT), (0, 0)))
    self_energy = box_sum(lax.optimization_barrier(jnp.sum(test_f * test_f, axis=-1)))

    def shifted(index):
        row_off = (index // side).astype(jnp.int32)
        col_off = (index % side).astype(jnp.int32)
        return lax.dynamic_slice(padded, (row_off, col_off, jnp.int32(0)), (height, width, chans))

    def logit(index):
        moved = shifted(index)
        cross = box_sum(lax.optimization_barrier(jnp.sum(test_f * moved, axis=-1)))
        other = box_sum(lax.optimization_barrier(jnp.sum(moved * moved, axis=-1)))
        return 32.0 * cross / jnp.sqrt(self_energy * other + 1e-05)
    shift_ids = jnp.arange(side * side, dtype=jnp.int32)
    logits = lax.map(logit, shift_ids)
    expo = jnp.exp(logits)
    weights = expo / lax.optimization_barrier(jnp.sum(expo, axis=0))

    def accumulate(total, pair):
        index, weight = pair
        return (total + weight[:, :, None] * shifted(index), None)
    aligned, _ = lax.scan(accumulate, jnp.zeros((height, width, chans), jnp.float32), (shift_ids, weights))
    return aligned

def conv_three(tile, kernel):
    height, width, chans = tile.shape
    padded = jnp.pad(tile, ((1, 1), (1, 1), (0, 0)))
    total = jnp.zeros((height * width, kernel.shape[1]), jnp.float32)
    for tap in range(9):
        row_off = tap // 3
        col_off = tap % 3
        window = padded[row_off:row_off + height, col_off:col_off + width].reshape(height * width, chans)
        total = total + jnp.dot(window, kernel[tap * chans:(tap + 1) * chans], preferred_element_type=jnp.float32)
    return total.reshape(height, width, kernel.shape[1])

def inspect_die(test_tile, golden_tile, kernels):
    aligned = align_golden(test_tile, golden_tile)
    residual = (test_tile.astype(jnp.float32) - aligned).astype(jnp.bfloat16)
    hidden = jax.nn.relu(conv_three(residual, kernels[0])).astype(jnp.bfloat16)
    refined = residual.astype(jnp.float32) + conv_three(hidden, kernels[1])
    return lax.optimization_barrier(jnp.mean(refined * refined, axis=-1))

def reference(features, zone_ids, golden_owner, defect_mask, kernels):

    def one_die(die):
        test_tile = features[die].reshape(H, W, C)
        golden_tile = features[golden_owner[zone_ids[die]]].reshape(H, W, C)
        return inspect_die(test_tile, golden_tile, kernels)
    energy = lax.map(one_die, jnp.arange(DIES, dtype=jnp.int32))
    masked = defect_mask.astype(jnp.float32)
    die_sum = lax.optimization_barrier(jnp.sum(energy * masked, axis=(1, 2)))
    die_count = lax.optimization_barrier(jnp.sum(masked, axis=(1, 2)))
    onehot = (zone_ids[:, None] == jnp.arange(Z, dtype=jnp.int32)[None, :]).astype(jnp.float32)
    zone_sum = lax.optimization_barrier(jnp.sum(onehot * die_sum[:, None], axis=0))
    zone_count = lax.optimization_barrier(jnp.sum(onehot * die_count[:, None], axis=0))
    zone_mean = zone_sum / jnp.maximum(zone_count, 1.0)
    mine = lax.optimization_barrier(jnp.sum(onehot * zone_mean[None, :], axis=1))
    return energy / (mine[:, None, None] + 0.01)
```

```python
import functools

import jax
import jax.numpy as jnp
from jax import lax
from jax.experimental import pallas as pl
from jax.experimental.pallas import tpu as pltpu
from jax.sharding import PartitionSpec as P

C = 64
H = 8
W = 128
SHIFT = 6
REACH = 2
Z = 8
CHUNKS = 2
MESH = pl.DeviceIdType.MESH


def lane_box(v):
    lane = lax.broadcasted_iota(jnp.int32, v.shape, v.ndim - 1)
    total = v
    for d in range(1, REACH + 1):
        right = pltpu.roll(v, d, v.ndim - 1)
        left = pltpu.roll(v, W - d, v.ndim - 1)
        total = total + jnp.where(lane >= d, right, 0.0) + jnp.where(lane < W - d, left, 0.0)
    return total


def rotate_rows(v, bits, sign):
    for k in range(4):
        step = 1 << k
        moved = pltpu.roll(v, (16 - step) if sign < 0 else step, v.ndim - 2)
        v = jnp.where(bits[k], moved, v)
    return v


def conv_taps(tile_f, stack, weights):
    lane = lax.rem(lax.broadcasted_iota(jnp.int32, (C, H * W), 1), W)
    pixels = H * W
    left = jnp.where(lane >= 1, pltpu.roll(tile_f, 1, 1), 0.0).astype(jnp.bfloat16)
    right = jnp.where(lane < W - 1, pltpu.roll(tile_f, pixels - 1, 1), 0.0).astype(jnp.bfloat16)
    views = (left, tile_f.astype(jnp.bfloat16), right)
    zeros = jnp.zeros((C, W), jnp.bfloat16)
    for tap in range(9):
        dy = tap // 3 - 1
        v = views[tap % 3]
        rows = slice(tap * C, (tap + 1) * C)
        if dy == 0:
            stack[rows, :] = v
        elif dy < 0:
            stack[rows, 0:W] = zeros
            stack[rows, W:pixels] = v[:, 0 : pixels - W]
        else:
            stack[rows, 0 : pixels - W] = v[:, W:pixels]
            stack[rows, pixels - W : pixels] = zeros
    return jnp.dot(weights, stack[...], preferred_element_type=jnp.float32)


def to_pixels(pieces, rows, pixels):
    at = 0
    for piece in pieces:
        for j in range(piece.shape[1] // 128):
            rows[at : at + H, :] = piece[:, j * 128 : (j + 1) * 128].astype(jnp.float32)
            at += H
    pairs = W * C // 128
    for y in range(H):
        v = rows[pl.ds(y, pairs, stride=H), :]
        pixels[pl.ds(y * W, pairs, stride=2), :] = v
        pixels[pl.ds(y * W + 1, pairs, stride=2), :] = pltpu.roll(v, C, 1)
    return pixels[:, 0:C]


def whole_kernel(
    n,
    zone_ref, owner_ref, feat_ref, mask_ref, k_hbm, score_ref,
    tile, k_ref, slots, stage, gold, zones,
    rows, pixels, t_ref, cross, res, stack, part, parts,
    local, send1, recv1, send2, recv2, zsend, zrecv, part_send, part_recv,
):
    half = n // 2
    span = feat_ref.shape[2] // half
    sub = span // CHUNKS
    me = lax.axis_index("col")
    mp = lax.rem(me, half)
    base = me - mp

    tile_copy = pltpu.make_async_copy(feat_ref.at[0], tile, local.at[0])
    k_copy = pltpu.make_async_copy(k_hbm, k_ref, local.at[1])
    tile_copy.start()
    k_copy.start()

    barrier = pltpu.get_barrier_semaphore()
    for o in range(1, n):
        pl.semaphore_signal(
            barrier, inc=1, device_id={"col": lax.rem(me + o, n)}, device_id_type=MESH
        )

    def peer(o):
        return base + lax.rem(mp + o, half)

    def zone_copy(o):
        return pltpu.make_async_remote_copy(
            src_ref=zone_ref,
            dst_ref=zones.at[o],
            send_sem=zsend.at[o],
            recv_sem=zrecv.at[o],
            device_id={"col": peer(o)},
            device_id_type=MESH,
        )

    def spread(k, o):
        dev = lax.rem(me + o, n)
        at = pl.multiple_of(lax.rem(dev, half) * span + k * sub, 128)
        return pltpu.make_async_remote_copy(
            src_ref=feat_ref.at[0, :, pl.ds(at, sub)],
            dst_ref=slots[k].at[o],
            send_sem=send1.at[k, o],
            recv_sem=recv1.at[k, o],
            device_id={"col": dev},
            device_id_type=MESH,
        )

    def deliver(k, o):
        return pltpu.make_async_remote_copy(
            src_ref=stage.at[k, o],
            dst_ref=gold.at[k, mp],
            send_sem=send2.at[k, o],
            recv_sem=recv2.at[k, o],
            device_id={"col": peer(o)},
            device_id_type=MESH,
        )

    tile_copy.wait()
    test = to_pixels([tile[...]], rows, pixels)
    t_f = test.T
    t_ref[...] = t_f

    pl.semaphore_wait(barrier, n - 1)
    for o in range(1, half):
        zone_copy(o).start()
    for k in range(CHUNKS):
        for o in range(1, n):
            spread(k, o).start()
    for k in range(CHUNKS):
        at = pl.multiple_of(mp * span + k * sub, 128)
        slots[k][0] = tile[:, pl.ds(at, sub)]
    k_copy.wait()

    for o in range(1, half):
        zone_copy(o).wait_recv()
    picks = [owner_ref[zone_ref[0]]] + [owner_ref[zones[half - o, 0]] for o in range(1, half)]
    froms = [lax.rem(me - g + n, n) for g in picks]
    for k in range(CHUNKS):
        for o in range(1, n):
            spread(k, o).wait_recv()
        for o in range(1, half):
            stage[k, o] = slots[k][froms[o]]
            deliver(k, o).start()
        gold[k, mp] = slots[k][froms[0]]
    for k in range(CHUNKS):
        for o in range(1, half):
            deliver(k, o).wait_recv()

    g_f = to_pixels([gold[k, p] for p in range(half) for k in range(CHUNKS)], rows, pixels)
    g = g_f.astype(jnp.bfloat16)
    gt = g_f.T.astype(jnp.bfloat16)
    fold_row = lax.broadcasted_iota(jnp.int32, (8, 16, W), 0) * 16 + lax.broadcasted_iota(
        jnp.int32, (8, 16, W), 1
    )
    gap = fold_row - lax.broadcasted_iota(jnp.int32, (8, 16, W), 2)
    near = jnp.logical_and(gap >= -8, gap < 8)
    near_f = jnp.where(near, 1.0, 0.0)
    near_b = near_f.astype(jnp.bfloat16)

    def bits_of(shape):
        spin = lax.broadcasted_iota(jnp.int32, shape, len(shape) - 1) + 8
        return [((spin >> k) & 1) == 1 for k in range(4)]

    bits3 = bits_of((H, 16, W))

    def band(full):
        v = full.reshape(H, 8, 16, W)
        v = jnp.sum(v * near_f[None], axis=1)
        return lane_box(rotate_rows(v, bits3, -1))

    for y in range(H):
        gram = jnp.dot(g, t_ref[:, y * W : (y + 1) * W].astype(jnp.bfloat16), preferred_element_type=jnp.float32)
        cross[y] = band(gram)
    square = jnp.sum(g_f * g_f, axis=1, keepdims=True)
    other_rows = band(jnp.broadcast_to(square, (H * W, W)))
    others = [other_rows[r] for r in range(H)]

    t_f = t_ref[...]
    own = jnp.sum(t_f * t_f, axis=0, keepdims=True)
    own_rows = [own[:, y * W : (y + 1) * W] for y in range(H)]
    row_id = lax.broadcasted_iota(jnp.int32, (16, W), 0)
    used = jnp.logical_and(row_id >= 8 - SHIFT, row_id <= 8 + SHIFT)

    for y in range(H):
        lo_y, hi_y = max(0, y - REACH), min(H - 1, y + REACH)
        self_energy = own_rows[lo_y]
        for r in range(lo_y + 1, hi_y + 1):
            self_energy = self_energy + own_rows[r]
        self_energy = jnp.broadcast_to(lane_box(self_energy), (16, W))
        denom = jnp.zeros((16, W), jnp.float32)
        picked = {}
        for a in range(-SHIFT, SHIFT + 1):
            num = None
            oth = None
            for r in range(lo_y, hi_y + 1):
                if 0 <= r + a < H:
                    num = cross[r, r + a] if num is None else num + cross[r, r + a]
                    oth = others[r + a] if oth is None else oth + others[r + a]
            if num is None:
                expo = jnp.where(used, 1.0, 0.0)
            else:
                logit = (32.0 * num) * lax.rsqrt(self_energy * oth + 1e-05)
                expo = jnp.where(used, jnp.exp(logit), 0.0)
            denom = denom + expo
            if 0 <= y + a < H:
                picked[y + a] = expo
        stacked = jnp.stack(
            [picked[r] if r in picked else jnp.zeros((16, W), jnp.float32) for r in range(H)]
        )
        stacked = rotate_rows(stacked, bits3, 1)
        high = stacked.astype(jnp.bfloat16)
        low = (stacked - high.astype(jnp.float32)).astype(jnp.bfloat16)
        wide_high = (high[:, None] * near_b[None]).reshape(H * W, W)
        wide_low = (low[:, None] * near_b[None]).reshape(H * W, W)
        numer = jnp.dot(gt, wide_high, preferred_element_type=jnp.float32) + jnp.dot(
            gt, wide_low, preferred_element_type=jnp.float32
        )
        total = jnp.sum(denom, axis=0, keepdims=True)
        aligned = numer / total
        cols = slice(y * W, (y + 1) * W)
        res[:, cols] = (t_f[:, cols] - aligned).astype(jnp.bfloat16).astype(jnp.float32)

    residual = res[...]
    hidden = jnp.maximum(conv_taps(residual, stack, k_ref[0]), 0.0)
    hidden = hidden.astype(jnp.bfloat16).astype(jnp.float32)
    refined = residual + conv_taps(hidden, stack, k_ref[1])
    flat = jnp.sum(refined * refined, axis=0, keepdims=True) * (1.0 / C)
    energy = jnp.concatenate([flat[:, y * W : (y + 1) * W] for y in range(H)], axis=0)
    masked = mask_ref[0].astype(jnp.float32)
    die_sum = jnp.sum(jnp.sum(energy * masked, axis=1, keepdims=True), axis=0, keepdims=True)
    die_count = jnp.sum(jnp.sum(masked, axis=1, keepdims=True), axis=0, keepdims=True)
    lane = lax.broadcasted_iota(jnp.int32, (1, W), 1)
    zone = zone_ref[0]
    at_sum = lane == zone
    at_count = lane == zone + W // 2
    mine = jnp.where(at_sum, die_sum, jnp.where(at_count, die_count, 0.0))
    part[...] = mine

    def give(k):
        return pltpu.make_async_remote_copy(
            src_ref=part,
            dst_ref=parts.at[k],
            send_sem=part_send.at[k],
            recv_sem=part_recv.at[k],
            device_id={"col": lax.rem(me + k, n)},
            device_id_type=MESH,
        )

    for k in range(1, n):
        give(k).start()

    for o in range(1, half):
        zone_copy(o).wait_send()
    for k in range(CHUNKS):
        for o in range(1, n):
            spread(k, o).wait_send()
        for o in range(1, half):
            deliver(k, o).wait_send()

    for k in range(1, n):
        give(k).wait_recv()
    total = mine
    for k in range(1, n):
        total = total + parts[k]
    zone_sum = jnp.sum(jnp.where(at_sum, total, 0.0), axis=1, keepdims=True)
    zone_count = jnp.sum(jnp.where(at_count, total, 0.0), axis=1, keepdims=True)
    mean = zone_sum / jnp.maximum(zone_count, 1.0)
    score_ref[0] = energy / (mean + 0.01)
    for k in range(1, n):
        give(k).wait_send()


def body(n, features, zone_ids, golden_owner, defect_mask, kernels):
    half = n // 2
    sub = W * C // half // CHUNKS
    vmem = pl.BlockSpec(memory_space=pltpu.VMEM)
    smem = pl.BlockSpec(memory_space=pltpu.SMEM)
    hbm = pl.BlockSpec(memory_space=pl.ANY)
    dma = pltpu.SemaphoreType.DMA
    return pl.pallas_call(
        functools.partial(whole_kernel, n),
        out_shape=jax.ShapeDtypeStruct((1, H, W), jnp.float32),
        in_specs=[smem, smem, hbm, vmem, hbm],
        out_specs=vmem,
        scratch_shapes=[
            pltpu.VMEM((H, W * C), jnp.bfloat16),
            pltpu.VMEM((2, C, 9 * C), jnp.bfloat16),
            [pltpu.VMEM((n, H, sub), jnp.bfloat16)] * CHUNKS,
            pltpu.VMEM((CHUNKS, half, H, sub), jnp.bfloat16),
            pltpu.VMEM((CHUNKS, half, H, sub), jnp.bfloat16),
            pltpu.SMEM((half, 1), jnp.int32),
            pltpu.VMEM((H * W * C // 128, 128), jnp.float32),
            pltpu.VMEM((H * W, 128), jnp.float32),
            pltpu.VMEM((C, H * W), jnp.float32),
            pltpu.VMEM((H, H, 16, W), jnp.float32),
            pltpu.VMEM((C, H * W), jnp.float32),
            pltpu.VMEM((9 * C, H * W), jnp.bfloat16),
            pltpu.VMEM((1, W), jnp.float32),
            pltpu.VMEM((n, 1, W), jnp.float32),
            dma((2,)),
            dma((CHUNKS, n)),
            dma((CHUNKS, n)),
            dma((CHUNKS, half)),
            dma((CHUNKS, half)),
            dma((half,)),
            dma((half,)),
            dma((n,)),
            dma((n,)),
        ],
        compiler_params=pltpu.CompilerParams(collective_id=0, has_side_effects=True),
    )(zone_ids, golden_owner, features, defect_mask, jnp.swapaxes(kernels, 1, 2))


def solution(mesh):
    in_specs = (
        P(("groups", "col"), None, None),
        P(("groups", "col")),
        P("groups"),
        P(("groups", "col"), None, None),
        P(),
    )
    out_specs = P(("groups", "col"), None, None)
    run = functools.partial(body, mesh.shape["col"])
    return jax.shard_map(run, mesh=mesh, in_specs=in_specs, out_specs=out_specs, check_vma=False)
```

```python
import functools

import jax
import jax.numpy as jnp
from jax import lax
from jax.experimental import pallas as pl
from jax.experimental.pallas import tpu as pltpu
from jax.sharding import PartitionSpec as P

C = 64
H = 8
W = 128
SHIFT = 6
REACH = 2
CHUNKS = 2
BLOCK = 4
PAIR = 2 * C
MESH = pl.DeviceIdType.MESH


def lane_box(v):
    lane = lax.broadcasted_iota(jnp.int32, v.shape, v.ndim - 1)
    total = v
    for d in range(1, REACH + 1):
        right = pltpu.roll(v, d, v.ndim - 1)
        left = pltpu.roll(v, W - d, v.ndim - 1)
        total = total + jnp.where(lane >= d, right, 0.0) + jnp.where(lane < W - d, left, 0.0)
    return total


def diagonal_box(v):
    lane = lax.broadcasted_iota(jnp.int32, v.shape, v.ndim - 1)
    total = v
    for d in range(1, REACH + 1):
        back = pltpu.roll(pltpu.roll(v, d, v.ndim - 1), d, v.ndim - 2)
        ahead = pltpu.roll(pltpu.roll(v, W - d, v.ndim - 1), 16 - d, v.ndim - 2)
        total = total + jnp.where(lane >= d, back, 0.0) + jnp.where(lane < W - d, ahead, 0.0)
    return total


def conv_taps(tile_f, stack, weights):
    lane = lax.rem(lax.broadcasted_iota(jnp.int32, (C, H * W), 1), W)
    pixels = H * W
    left = jnp.where(lane >= 1, pltpu.roll(tile_f, 1, 1), 0.0).astype(jnp.bfloat16)
    right = jnp.where(lane < W - 1, pltpu.roll(tile_f, pixels - 1, 1), 0.0).astype(jnp.bfloat16)
    views = (left, tile_f.astype(jnp.bfloat16), right)
    zeros = jnp.zeros((C, W), jnp.bfloat16)
    for tap in range(9):
        dy = tap // 3 - 1
        v = views[tap % 3]
        rows = slice(tap * C, (tap + 1) * C)
        if dy == 0:
            stack[rows, :] = v
        elif dy < 0:
            stack[rows, 0:W] = zeros
            stack[rows, W:pixels] = v[:, 0 : pixels - W]
        else:
            stack[rows, 0 : pixels - W] = v[:, W:pixels]
            stack[rows, pixels - W : pixels] = zeros
    return jnp.dot(weights, stack[...], preferred_element_type=jnp.float32)


def to_pixels(pieces, rows, pixels):
    at = 0
    for piece in pieces:
        for j in range(piece.shape[1] // PAIR):
            rows[at : at + H, :] = piece[:, j * PAIR : (j + 1) * PAIR].astype(jnp.float32)
            at += H
    pairs = at // H
    for y in range(H):
        v = rows[pl.ds(y, pairs, stride=H), :]
        pixels[pl.ds(y * 2 * pairs, pairs, stride=2), :] = v
        pixels[pl.ds(y * 2 * pairs + 1, pairs, stride=2), :] = pltpu.roll(v, C, 1)
    return pixels[0 : H * 2 * pairs, 0:C]


def whole_kernel(
    n,
    zone_ref, owner_ref, feat_ref, mask_ref, k_hbm, score_ref,
    tile, k_ref, slots, stage, gold, zones,
    rows, pixels, t_ref, tb_ref, cross, res, stack, parts,
    gates, local, send1, recv1, send2, recv2, zsend, zrecv, part_send, part_recv,
):
    sub = W * C // CHUNKS // n
    run = 8 * C
    me = lax.axis_index("col")
    block = me // BLOCK

    tile_copy = pltpu.make_async_copy(feat_ref.at[0], tile, local.at[0])
    k_copy = pltpu.make_async_copy(k_hbm, k_ref, local.at[1])

    def start_of(k, p):
        lane = p * sub
        at = lane // run * (CHUNKS * run) + k * run + lax.rem(lane, run)
        return pl.multiple_of(at, PAIR)

    def remote(src, dst, send_sem, recv_sem, dev):
        return pltpu.make_async_remote_copy(
            src_ref=src,
            dst_ref=dst,
            send_sem=send_sem,
            recv_sem=recv_sem,
            device_id={"col": dev},
            device_id_type=MESH,
        )

    def zone_copy(dev):
        return remote(zone_ref, zones.at[me], zsend, zrecv, dev)

    def spread(k, dev):
        piece = feat_ref.at[0, :, pl.ds(start_of(k, dev), sub)]
        return remote(piece, slots[k].at[me], send1.at[k], recv1.at[k], dev)

    def deliver(k, dev):
        return remote(stage.at[k, dev], gold.at[k, me], send2.at[k], recv2.at[k], dev)

    def all_but_one(ref, send_sem, recv_sem):
        rest = ref.at[pl.ds(0, n - 1)]
        return remote(rest, rest, send_sem, recv_sem, lax.rem(me + 1, n))

    zone_all = all_but_one(zones, zsend, zrecv)
    spread_all = [all_but_one(slots[k], send1.at[k], recv1.at[k]) for k in range(CHUNKS)]
    deliver_all = [all_but_one(gold.at[k], send2.at[k], recv2.at[k]) for k in range(CHUNKS)]

    barrier = pltpu.get_barrier_semaphore()

    @pl.loop(me + 1, n)
    def _(dev):
        pl.semaphore_signal(barrier, inc=1, device_id={"col": dev}, device_id_type=MESH)

    tile_copy.start()
    k_copy.start()

    @pl.when(me > 0)
    def _():
        pl.semaphore_wait(barrier, me)

    @pl.loop(0, me)
    def _(dev):
        pl.semaphore_signal(gates.at[block], inc=1, device_id={"col": dev}, device_id_type=MESH)

    def send_to(dev):
        zone_copy(dev).start()
        for k in range(CHUNKS):
            spread(k, dev).start()

    @pl.loop(0, me)
    def _(dev):
        send_to(dev)

    tile_copy.wait()
    t_f = to_pixels([tile[...]], rows, pixels).T
    t_ref[...] = t_f
    tb_ref[...] = t_f.astype(jnp.bfloat16)
    for k in range(CHUNKS):
        slots[k][me] = tile[:, pl.ds(start_of(k, me), sub)]
    k_copy.wait()

    @pl.loop(block, n // BLOCK)
    def _(b):
        first = jnp.maximum(me + 1, b * BLOCK)
        last = (b + 1) * BLOCK

        @pl.when(last > first)
        def _():
            pl.semaphore_wait(gates.at[b], last - first)

        @pl.loop(first, last)
        def _(dev):
            send_to(dev)

    zone_all.wait_recv()
    for k in range(CHUNKS):
        spread_all[k].wait_recv()
        for o in range(1, n):
            dev = lax.rem(me + o, n)
            stage[k, dev] = slots[k][owner_ref[zones[dev, 0]]]
            deliver(k, dev).start()
        gold[k, me] = slots[k][owner_ref[zone_ref[0]]]

    row = lax.broadcasted_iota(jnp.int32, (8, W), 0)
    column = lax.broadcasted_iota(jnp.int32, (8, W), 1)

    def near(k, b):
        gap = 16 * b + 8 * k + row - column
        return jnp.logical_and(gap >= -8, gap < 8)

    def fold(k, v):
        v = v.reshape(H, 8, 8, W)
        total = jnp.zeros((H, 8, W), jnp.float32)
        for b in range(8):
            total = jnp.where(near(k, b)[None], v[:, b], total)
        return total

    t_b = tb_ref[...]
    gts = []
    squares = []
    for k in range(CHUNKS):
        deliver_all[k].wait_recv()
        g_f = to_pixels([gold[k, p] for p in range(n)], rows, pixels)
        g = g_f.astype(jnp.bfloat16)
        gts.append(g_f.T.astype(jnp.bfloat16))
        for y in range(0, H, 2):
            gram = jnp.dot(g, t_b[:, y * W : (y + 2) * W], preferred_element_type=jnp.float32)
            for i in range(2):
                cross[y + i, :, 8 * k : 8 * k + 8, :] = fold(k, gram[:, i * W : (i + 1) * W])
        square = jnp.sum(g_f * g_f, axis=1, keepdims=True)
        squares.append(fold(k, jnp.broadcast_to(square, (H * W // CHUNKS, W))))
    gt = jnp.concatenate(gts, axis=1)
    for y in range(H):
        cross[y] = diagonal_box(cross[y])
    other_rows = diagonal_box(jnp.concatenate(squares, axis=1))
    windows = {}

    def other_window(lo, hi):
        lo, hi = max(lo, 0), min(hi, H - 1)
        if (lo, hi) not in windows:
            total = other_rows[lo]
            for r in range(lo + 1, hi + 1):
                total = total + other_rows[r]
            windows[lo, hi] = total
        return windows[lo, hi]

    t_f = t_ref[...]
    own = jnp.sum(t_f * t_f, axis=0, keepdims=True)
    own_rows = [own[:, y * W : (y + 1) * W] for y in range(H)]
    slot = lax.broadcasted_iota(jnp.int32, (16, W), 0)
    shift = lax.rem(slot - lax.broadcasted_iota(jnp.int32, (16, W), 1) + W + 8, 16) - 8
    used = jnp.logical_and(shift >= -SHIFT, shift <= SHIFT)

    for y in range(H):
        lo_y, hi_y = max(0, y - REACH), min(H - 1, y + REACH)
        self_energy = own_rows[lo_y]
        for r in range(lo_y + 1, hi_y + 1):
            self_energy = self_energy + own_rows[r]
        self_energy = jnp.broadcast_to(lane_box(self_energy), (16, W))
        denom = jnp.zeros((16, W), jnp.float32)
        picked = {}
        for a in range(-SHIFT, SHIFT + 1):
            num = None
            for r in range(lo_y, hi_y + 1):
                if 0 <= r + a < H:
                    num = cross[r, r + a] if num is None else num + cross[r, r + a]
            if num is None:
                expo = jnp.where(used, 1.0, 0.0)
            else:
                oth = other_window(lo_y + a, hi_y + a)
                logit = (32.0 * num) * lax.rsqrt(self_energy * oth + 1e-05)
                expo = jnp.where(used, jnp.exp(logit), 0.0)
            denom = denom + expo
            if 0 <= y + a < H:
                picked[y + a] = expo
        wides = []
        for k in range(CHUNKS):
            for r in range(H):
                for b in range(8):
                    if r in picked:
                        wides.append(jnp.where(near(k, b), picked[r][8 * k : 8 * k + 8], 0.0))
                    else:
                        wides.append(jnp.zeros((8, W), jnp.float32))
        wide = jnp.concatenate(wides, axis=0)
        high = wide.astype(jnp.bfloat16)
        low = (wide - high.astype(jnp.float32)).astype(jnp.bfloat16)
        both = jnp.dot(gt, jnp.concatenate([high, low], axis=1), preferred_element_type=jnp.float32)
        numer = both[:, 0:W] + both[:, W : 2 * W]
        total = jnp.sum(denom, axis=0, keepdims=True)
        aligned = numer / total
        cols = slice(y * W, (y + 1) * W)
        res[:, cols] = (t_f[:, cols] - aligned).astype(jnp.bfloat16).astype(jnp.float32)

    residual = res[...]
    hidden = jnp.maximum(conv_taps(residual, stack, k_ref[0]), 0.0)
    hidden = hidden.astype(jnp.bfloat16).astype(jnp.float32)
    refined = residual + conv_taps(hidden, stack, k_ref[1])
    flat = jnp.sum(refined * refined, axis=0, keepdims=True) * (1.0 / C)
    energy = jnp.concatenate([flat[:, y * W : (y + 1) * W] for y in range(H)], axis=0)
    masked = mask_ref[0].astype(jnp.float32)
    die_sum = jnp.sum(jnp.sum(energy * masked, axis=1, keepdims=True), axis=0, keepdims=True)
    die_count = jnp.sum(jnp.sum(masked, axis=1, keepdims=True), axis=0, keepdims=True)
    lane = lax.broadcasted_iota(jnp.int32, (1, W), 1)
    zone = zone_ref[0]
    at_sum = lane == zone
    at_count = lane == zone + W // 2
    parts[0] = jnp.where(at_sum, die_sum, jnp.where(at_count, die_count, 0.0))

    def give(k):
        return remote(parts.at[0], parts.at[k], part_send, part_recv, lax.rem(me + k, n))

    for k in range(1, n):
        give(k).start()

    zone_all.wait_send()
    for k in range(CHUNKS):
        spread_all[k].wait_send()
        deliver_all[k].wait_send()

    rest = parts.at[pl.ds(1, n - 1)]
    give_all = remote(rest, rest, part_send, part_recv, lax.rem(me + 1, n))
    give_all.wait_recv()
    total = jnp.sum(parts[...], axis=0)
    zone_sum = jnp.sum(jnp.where(at_sum, total, 0.0), axis=1, keepdims=True)
    zone_count = jnp.sum(jnp.where(at_count, total, 0.0), axis=1, keepdims=True)
    mean = zone_sum / jnp.maximum(zone_count, 1.0)
    score_ref[0] = energy / (mean + 0.01)
    give_all.wait_send()


def body(n, features, zone_ids, golden_owner, defect_mask, kernels):
    sub = W * C // CHUNKS // n
    vmem = pl.BlockSpec(memory_space=pltpu.VMEM)
    smem = pl.BlockSpec(memory_space=pltpu.SMEM)
    hbm = pl.BlockSpec(memory_space=pl.ANY)
    dma = pltpu.SemaphoreType.DMA
    return pl.pallas_call(
        functools.partial(whole_kernel, n),
        out_shape=jax.ShapeDtypeStruct((1, H, W), jnp.float32),
        in_specs=[smem, smem, hbm, vmem, hbm],
        out_specs=vmem,
        scratch_shapes=[
            pltpu.VMEM((H, W * C), jnp.bfloat16),
            pltpu.VMEM((2, C, 9 * C), jnp.bfloat16),
            [pltpu.VMEM((n, H, sub), jnp.bfloat16)] * CHUNKS,
            pltpu.VMEM((CHUNKS, n, H, sub), jnp.bfloat16),
            pltpu.VMEM((CHUNKS, n, H, sub), jnp.bfloat16),
            pltpu.SMEM((n, 1), jnp.int32),
            pltpu.VMEM((H * W * C // 128, 128), jnp.float32),
            pltpu.VMEM((H * W, 128), jnp.float32),
            pltpu.VMEM((C, H * W), jnp.float32),
            pltpu.VMEM((C, H * W), jnp.bfloat16),
            pltpu.VMEM((H, H, 16, W), jnp.float32),
            pltpu.VMEM((C, H * W), jnp.float32),
            pltpu.VMEM((9 * C, H * W), jnp.bfloat16),
            pltpu.VMEM((n, 1, W), jnp.float32),
            pltpu.SemaphoreType.REGULAR((n // BLOCK,)),
            dma((2,)),
            dma((CHUNKS,)),
            dma((CHUNKS,)),
            dma((CHUNKS,)),
            dma((CHUNKS,)),
            dma,
            dma,
            dma,
            dma,
        ],
        compiler_params=pltpu.CompilerParams(collective_id=0, has_side_effects=True),
    )(zone_ids, golden_owner, features, defect_mask, jnp.swapaxes(kernels, 1, 2))


def solution(mesh):
    in_specs = (
        P(("groups", "col"), None, None),
        P(("groups", "col")),
        P("groups"),
        P(("groups", "col"), None, None),
        P(),
    )
    out_specs = P(("groups", "col"), None, None)
    run = functools.partial(body, mesh.shape["col"])
    return jax.shard_map(run, mesh=mesh, in_specs=in_specs, out_specs=out_specs, check_vma=False)
```

```python
import functools

import jax
import jax.numpy as jnp
from jax import lax
from jax.experimental import pallas as pl
from jax.experimental.pallas import tpu as pltpu
from jax.sharding import PartitionSpec as P

C = 64
H = 8
W = 128
SHIFT = 6
REACH = 2
FOLDS = 2
BLOCK = 4
PAIR = 2 * C
MESH = pl.DeviceIdType.MESH


def lane_box(v):
    lane = lax.broadcasted_iota(jnp.int32, v.shape, v.ndim - 1)
    total = v
    for d in range(1, REACH + 1):
        right = pltpu.roll(v, d, v.ndim - 1)
        left = pltpu.roll(v, W - d, v.ndim - 1)
        total = total + jnp.where(lane >= d, right, 0.0) + jnp.where(lane < W - d, left, 0.0)
    return total


def diagonal_box(v):
    lane = lax.broadcasted_iota(jnp.int32, v.shape, v.ndim - 1)
    total = v
    for d in range(1, REACH + 1):
        back = pltpu.roll(pltpu.roll(v, d, v.ndim - 1), d, v.ndim - 2)
        ahead = pltpu.roll(pltpu.roll(v, W - d, v.ndim - 1), 16 - d, v.ndim - 2)
        total = total + jnp.where(lane >= d, back, 0.0) + jnp.where(lane < W - d, ahead, 0.0)
    return total


def conv_taps(tile_f, stack, weights):
    lane = lax.rem(lax.broadcasted_iota(jnp.int32, (C, H * W), 1), W)
    pixels = H * W
    left = jnp.where(lane >= 1, pltpu.roll(tile_f, 1, 1), 0.0).astype(jnp.bfloat16)
    right = jnp.where(lane < W - 1, pltpu.roll(tile_f, pixels - 1, 1), 0.0).astype(jnp.bfloat16)
    views = (left, tile_f.astype(jnp.bfloat16), right)
    zeros = jnp.zeros((C, W), jnp.bfloat16)
    for tap in range(9):
        dy = tap // 3 - 1
        v = views[tap % 3]
        rows = slice(tap * C, (tap + 1) * C)
        if dy == 0:
            stack[rows, :] = v
        elif dy < 0:
            stack[rows, 0:W] = zeros
            stack[rows, W:pixels] = v[:, 0 : pixels - W]
        else:
            stack[rows, 0 : pixels - W] = v[:, W:pixels]
            stack[rows, pixels - W : pixels] = zeros
    return jnp.dot(weights, stack[...], preferred_element_type=jnp.float32)


def to_pixels(tiles, rows, pixels):
    for at, tile in enumerate(tiles):
        rows[at * H : (at + 1) * H, :] = tile.astype(jnp.float32)
    pairs = len(tiles)
    for y in range(H):
        v = rows[pl.ds(y, pairs, stride=H), :]
        pixels[pl.ds(y * 2 * pairs, pairs, stride=2), :] = v
        pixels[pl.ds(y * 2 * pairs + 1, pairs, stride=2), :] = pltpu.roll(v, C, 1)
    return pixels[0 : H * 2 * pairs, 0:C]


def whole_kernel(
    n,
    zone_hbm, owner_hbm, feat_ref, mask_hbm, k_hbm, score_ref,
    zone_ref, owner_ref, mask_ref, tile, k_ref, slots, stage, gold, zones,
    rows, pixels, t_ref, tb_ref, cross, res, stack, parts,
    gates, local, send1, recv1, send2, recv2, zsend, zrecv, part_send, part_recv,
):
    half = n // 2
    low_home, end_home = n // 4, n // 4 + half
    sub = W * C // half
    me = lax.axis_index("col")
    block = me // BLOCK
    is_home = jnp.logical_and(me >= low_home, me < end_home)
    not_home = jnp.logical_not(is_home)
    mine = me - low_home

    tile_copy = pltpu.make_async_copy(feat_ref.at[0], tile, local.at[0])
    k_copy = pltpu.make_async_copy(k_hbm, k_ref, local.at[1])
    mask_copy = pltpu.make_async_copy(mask_hbm, mask_ref, local.at[2])
    zone_load = pltpu.make_async_copy(zone_hbm, zone_ref, local.at[3])
    owner_load = pltpu.make_async_copy(owner_hbm, owner_ref, local.at[4])
    tile_copy.start()
    zone_load.start()

    def part_of(p):
        return pl.ds(pl.multiple_of(p * sub, PAIR), sub)

    def remote(src, dst, send_sem, recv_sem, dev):
        return pltpu.make_async_remote_copy(
            src_ref=src,
            dst_ref=dst,
            send_sem=send_sem,
            recv_sem=recv_sem,
            device_id={"col": dev},
            device_id_type=MESH,
        )

    def zone_copy(dev):
        return remote(zone_ref, zones.at[me], zsend, zrecv, dev)

    def spread(dev):
        return remote(tile.at[:, part_of(dev - low_home)], slots.at[me], send1, recv1, dev)

    def deliver(dev):
        return remote(stage.at[dev], gold.at[mine], send2, recv2, dev)

    def several(ref, count, send_sem, recv_sem):
        rest = ref.at[pl.ds(0, count)]
        return remote(rest, rest, send_sem, recv_sem, lax.rem(me + 1, n))

    def wait_homes(wait):
        @pl.when(is_home)
        def _():
            wait(half - 1)

        @pl.when(not_home)
        def _():
            wait(half)

    barrier = pltpu.get_barrier_semaphore()

    first_later = jnp.where(is_home, me + 1, jnp.maximum(me + 1, low_home))
    end_later = jnp.where(is_home, n, jnp.maximum(first_later, end_home))

    @pl.loop(first_later, end_later)
    def _(dev):
        pl.semaphore_signal(barrier, inc=1, device_id={"col": dev}, device_id_type=MESH)

    k_copy.start()
    mask_copy.start()
    owner_load.start()
    zone_load.wait()
    tile_copy.wait()

    greetings = jnp.where(is_home, me, jnp.where(me < low_home, 0, half))

    @pl.when(greetings > 0)
    def _():
        pl.semaphore_wait(barrier, greetings)

    @pl.when(is_home)
    def _():
        @pl.loop(0, me)
        def _(dev):
            pl.semaphore_signal(gates.at[block], inc=1, device_id={"col": dev}, device_id_type=MESH)

    def send_to(first, last):
        @pl.loop(first, last)
        def _(dev):
            spread(dev).start()

        @pl.loop(first, last)
        def _(dev):
            zone_copy(dev).start()

    send_to(low_home, jnp.clip(me, low_home, end_home))
    lanes = [slice(t * PAIR, (t + 1) * PAIR) for t in range(W * C // PAIR)]
    t_f = to_pixels([tile[:, at] for at in lanes], rows, pixels).T
    t_ref[...] = t_f
    tb_ref[...] = t_f.astype(jnp.bfloat16)

    @pl.when(is_home)
    def _():
        slots[me] = tile[:, part_of(mine)]

    k_copy.wait()
    mask_copy.wait()
    owner_load.wait()

    for b in range(low_home // BLOCK, end_home // BLOCK):
        first = jnp.maximum(me + 1, b * BLOCK)
        last = (b + 1) * BLOCK

        @pl.when(last > first)
        def _():
            pl.semaphore_wait(gates.at[b], last - first)
            send_to(first, last)

    @pl.when(is_home)
    def _():
        several(zones, n - 1, zsend, zrecv).wait_recv()
        wanted = [lax.rem(me + o, n) for o in range(1, n)]
        wanted = [(dev, owner_ref[zones[dev, 0]]) for dev in wanted]
        several(slots, n - 1, send1, recv1).wait_recv()
        for dev, owner in wanted:
            stage[dev] = slots[owner]
            deliver(dev).start()
        gold[mine] = slots[owner_ref[zone_ref[0]]]

    row = lax.broadcasted_iota(jnp.int32, (8, W), 0)
    column = lax.broadcasted_iota(jnp.int32, (8, W), 1)

    def near(k, b):
        gap = 16 * b + 8 * k + row - column
        return jnp.logical_and(gap >= -8, gap < 8)

    def fold(k, v):
        v = v.reshape(H, 8, 8, W)
        total = jnp.zeros((H, 8, W), jnp.float32)
        for b in range(8):
            total = jnp.where(near(k, b)[None], v[:, b], total)
        return total

    t_b = tb_ref[...]
    gts = []
    squares = []
    wait_homes(lambda count: several(gold, count, send2, recv2).wait_recv())
    for k in range(FOLDS):
        tiles = [(b * FOLDS + k) * (8 // 2) + t for b in range(8) for t in range(8 // 2)]
        places = [(t * PAIR // sub, t * PAIR % sub) for t in tiles]
        g_f = to_pixels([gold[p, :, at : at + PAIR] for p, at in places], rows, pixels)
        g = g_f.astype(jnp.bfloat16)
        gts.append(g_f.T.astype(jnp.bfloat16))
        for y in range(0, H, 2):
            gram = jnp.dot(g, t_b[:, y * W : (y + 2) * W], preferred_element_type=jnp.float32)
            for i in range(2):
                cross[y + i, :, 8 * k : 8 * k + 8, :] = fold(k, gram[:, i * W : (i + 1) * W])
        square = jnp.sum(g_f * g_f, axis=1, keepdims=True)
        squares.append(fold(k, jnp.broadcast_to(square, (H * W // FOLDS, W))))
    gt = jnp.concatenate(gts, axis=1)
    for y in range(H):
        cross[y] = diagonal_box(cross[y])
    other_rows = diagonal_box(jnp.concatenate(squares, axis=1))
    windows = {}

    def other_window(lo, hi):
        lo, hi = max(lo, 0), min(hi, H - 1)
        if (lo, hi) not in windows:
            total = other_rows[lo]
            for r in range(lo + 1, hi + 1):
                total = total + other_rows[r]
            windows[lo, hi] = total
        return windows[lo, hi]

    t_f = t_ref[...]
    own = jnp.sum(t_f * t_f, axis=0, keepdims=True)
    own_rows = [own[:, y * W : (y + 1) * W] for y in range(H)]
    slot = lax.broadcasted_iota(jnp.int32, (16, W), 0)
    shift = lax.rem(slot - lax.broadcasted_iota(jnp.int32, (16, W), 1) + W + 8, 16) - 8
    used = jnp.logical_and(shift >= -SHIFT, shift <= SHIFT)

    for y in range(H):
        lo_y, hi_y = max(0, y - REACH), min(H - 1, y + REACH)
        self_energy = own_rows[lo_y]
        for r in range(lo_y + 1, hi_y + 1):
            self_energy = self_energy + own_rows[r]
        self_energy = jnp.broadcast_to(lane_box(self_energy), (16, W))
        denom = jnp.zeros((16, W), jnp.float32)
        picked = {}
        for a in range(-SHIFT, SHIFT + 1):
            num = None
            for r in range(lo_y, hi_y + 1):
                if 0 <= r + a < H:
                    num = cross[r, r + a] if num is None else num + cross[r, r + a]
            if num is None:
                expo = jnp.where(used, 1.0, 0.0)
            else:
                oth = other_window(lo_y + a, hi_y + a)
                logit = (32.0 * num) * lax.rsqrt(self_energy * oth + 1e-05)
                expo = jnp.where(used, jnp.exp(logit), 0.0)
            denom = denom + expo
            if 0 <= y + a < H:
                picked[y + a] = expo
        wides = []
        for k in range(FOLDS):
            for r in range(H):
                for b in range(8):
                    if r in picked:
                        wides.append(jnp.where(near(k, b), picked[r][8 * k : 8 * k + 8], 0.0))
                    else:
                        wides.append(jnp.zeros((8, W), jnp.float32))
        wide = jnp.concatenate(wides, axis=0)
        high = wide.astype(jnp.bfloat16)
        low = (wide - high.astype(jnp.float32)).astype(jnp.bfloat16)
        both = jnp.dot(gt, jnp.concatenate([high, low], axis=1), preferred_element_type=jnp.float32)
        numer = both[:, 0:W] + both[:, W : 2 * W]
        total = jnp.sum(denom, axis=0, keepdims=True)
        aligned = numer / total
        cols = slice(y * W, (y + 1) * W)
        res[:, cols] = (t_f[:, cols] - aligned).astype(jnp.bfloat16).astype(jnp.float32)

    residual = res[...]
    hidden = jnp.maximum(conv_taps(residual, stack, k_ref[0]), 0.0)
    hidden = hidden.astype(jnp.bfloat16).astype(jnp.float32)
    refined = residual + conv_taps(hidden, stack, k_ref[1])
    flat = jnp.sum(refined * refined, axis=0, keepdims=True) * (1.0 / C)
    energy = jnp.concatenate([flat[:, y * W : (y + 1) * W] for y in range(H)], axis=0)
    masked = mask_ref[0].astype(jnp.float32)
    die_sum = jnp.sum(jnp.sum(energy * masked, axis=1, keepdims=True), axis=0, keepdims=True)
    die_count = jnp.sum(jnp.sum(masked, axis=1, keepdims=True), axis=0, keepdims=True)
    lane = lax.broadcasted_iota(jnp.int32, (1, W), 1)
    zone = zone_ref[0]
    at_sum = lane == zone
    at_count = lane == zone + W // 2
    parts[0] = jnp.where(at_sum, die_sum, jnp.where(at_count, die_count, 0.0))

    def give(k):
        return remote(parts.at[0], parts.at[k], part_send, part_recv, lax.rem(me + k, n))

    for k in range(1, n):
        give(k).start()

    wait_homes(lambda count: several(zones, count, zsend, zrecv).wait_send())
    wait_homes(lambda count: several(slots, count, send1, recv1).wait_send())

    @pl.when(is_home)
    def _():
        several(stage, n - 1, send2, recv2).wait_send()

    rest = parts.at[pl.ds(1, n - 1)]
    give_all = remote(rest, rest, part_send, part_recv, lax.rem(me + 1, n))
    give_all.wait_recv()
    total = jnp.sum(parts[...], axis=0)
    zone_sum = jnp.sum(jnp.where(at_sum, total, 0.0), axis=1, keepdims=True)
    zone_count = jnp.sum(jnp.where(at_count, total, 0.0), axis=1, keepdims=True)
    mean = zone_sum / jnp.maximum(zone_count, 1.0)
    score_ref[0] = energy / (mean + 0.01)
    give_all.wait_send()


def body(n, features, zone_ids, golden_owner, defect_mask, kernels):
    half = n // 2
    sub = W * C // half
    vmem = pl.BlockSpec(memory_space=pltpu.VMEM)
    hbm = pl.BlockSpec(memory_space=pl.ANY)
    dma = pltpu.SemaphoreType.DMA
    return pl.pallas_call(
        functools.partial(whole_kernel, n),
        out_shape=jax.ShapeDtypeStruct((1, H, W), jnp.float32),
        in_specs=[hbm] * 5,
        out_specs=vmem,
        scratch_shapes=[
            pltpu.SMEM((1,), jnp.int32),
            pltpu.SMEM(golden_owner.shape, jnp.int32),
            pltpu.VMEM((1, H, W), jnp.int32),
            pltpu.VMEM((H, W * C), jnp.bfloat16),
            pltpu.VMEM((2, C, 9 * C), jnp.bfloat16),
            pltpu.VMEM((n, H, sub), jnp.bfloat16),
            pltpu.VMEM((n, H, sub), jnp.bfloat16),
            pltpu.VMEM((half, H, sub), jnp.bfloat16),
            pltpu.SMEM((n, 1), jnp.int32),
            pltpu.VMEM((H * W * C // 128, 128), jnp.float32),
            pltpu.VMEM((H * W, 128), jnp.float32),
            pltpu.VMEM((C, H * W), jnp.float32),
            pltpu.VMEM((C, H * W), jnp.bfloat16),
            pltpu.VMEM((H, H, 16, W), jnp.float32),
            pltpu.VMEM((C, H * W), jnp.float32),
            pltpu.VMEM((9 * C, H * W), jnp.bfloat16),
            pltpu.VMEM((n, 1, W), jnp.float32),
            pltpu.SemaphoreType.REGULAR((n // BLOCK,)),
            dma((5,)),
            dma,
            dma,
            dma,
            dma,
            dma,
            dma,
            dma,
            dma,
        ],
        compiler_params=pltpu.CompilerParams(collective_id=0, has_side_effects=True),
    )(zone_ids, golden_owner, features, defect_mask, jnp.swapaxes(kernels, 1, 2))


def solution(mesh):
    in_specs = (
        P(("groups", "col"), None, None),
        P(("groups", "col")),
        P("groups"),
        P(("groups", "col"), None, None),
        P(),
    )
    out_specs = P(("groups", "col"), None, None)
    run = functools.partial(body, mesh.shape["col"])
    return jax.shard_map(run, mesh=mesh, in_specs=in_specs, out_specs=out_specs, check_vma=False)
```

```python
import functools
import math

import jax
import jax.numpy as jnp
from jax import lax
from jax.experimental import pallas as pl
from jax.experimental.pallas import tpu as pltpu
from jax.sharding import PartitionSpec as P

C = 64
H = 8
W = 128
SHIFT = 6
REACH = 2
FOLDS = 2
BLOCK = 4
PAIR = 2 * C
SCALE = 32.0 * math.log2(math.e)
MESH = pl.DeviceIdType.MESH


def lane_box(v):
    lane = lax.broadcasted_iota(jnp.int32, v.shape, v.ndim - 1)
    total = v
    for d in range(1, REACH + 1):
        right = pltpu.roll(v, d, v.ndim - 1)
        left = pltpu.roll(v, W - d, v.ndim - 1)
        total = total + jnp.where(lane >= d, right, 0.0) + jnp.where(lane < W - d, left, 0.0)
    return total


def diagonal_box(v):
    lane = lax.broadcasted_iota(jnp.int32, v.shape, v.ndim - 1)
    total = v
    for d in range(1, REACH + 1):
        back = pltpu.roll(pltpu.roll(v, d, v.ndim - 1), d, v.ndim - 2)
        ahead = pltpu.roll(pltpu.roll(v, W - d, v.ndim - 1), 16 - d, v.ndim - 2)
        total = total + jnp.where(lane >= d, back, 0.0) + jnp.where(lane < W - d, ahead, 0.0)
    return total


def conv_rows(tile_f, views, weights):
    lane = lax.rem(lax.broadcasted_iota(jnp.int32, (C, H * W), 1), W)
    pixels = H * W
    views[0:C, :] = jnp.where(lane >= 1, pltpu.roll(tile_f, 1, 1), 0.0).astype(jnp.bfloat16)
    views[C : 2 * C, :] = tile_f.astype(jnp.bfloat16)
    right = jnp.where(lane < W - 1, pltpu.roll(tile_f, pixels - 1, 1), 0.0)
    views[2 * C : 3 * C, :] = right.astype(jnp.bfloat16)
    sums = jnp.dot(weights, views[...], preferred_element_type=jnp.float32)
    zeros = jnp.zeros((C, W), jnp.float32)
    above = jnp.concatenate([zeros, sums[0:C, 0 : pixels - W]], axis=1)
    below = jnp.concatenate([sums[2 * C : 3 * C, W:pixels], zeros], axis=1)
    return above + sums[C : 2 * C] + below


def to_pixels(tiles, rows, pixels):
    for at, tile in enumerate(tiles):
        rows[at * H : (at + 1) * H, :] = tile.astype(jnp.float32)
    pairs = len(tiles)
    for y in range(H):
        v = rows[pl.ds(y, pairs, stride=H), :]
        pixels[pl.ds(y * 2 * pairs, pairs, stride=2), :] = v
        pixels[pl.ds(y * 2 * pairs + 1, pairs, stride=2), :] = pltpu.roll(v, C, 1)
    return pixels[0 : H * 2 * pairs, 0:C]


def whole_kernel(
    n,
    zone_hbm, owner_hbm, feat_ref, mask_hbm, k_hbm, score_ref,
    zone_ref, owner_ref, mask_ref, tile, k_ref, w_ref, slots, stage, gold, zones,
    rows, pixels, t_ref, tb_ref, cross, res, stack, parts,
    gates, local, send1, recv1, send2, recv2, zsend, zrecv, part_send, part_recv,
):
    half = n // 2
    low_home, end_home = n // 4, n // 4 + half
    sub = W * C // half
    me = lax.axis_index("col")
    block = me // BLOCK
    is_home = jnp.logical_and(me >= low_home, me < end_home)
    not_home = jnp.logical_not(is_home)
    mine = me - low_home

    tile_copy = pltpu.make_async_copy(feat_ref.at[0], tile, local.at[0])
    k_copy = pltpu.make_async_copy(k_hbm, k_ref, local.at[1])
    mask_copy = pltpu.make_async_copy(mask_hbm, mask_ref, local.at[2])
    zone_load = pltpu.make_async_copy(zone_hbm, zone_ref, local.at[3])
    owner_load = pltpu.make_async_copy(owner_hbm, owner_ref, local.at[4])
    tile_copy.start()
    zone_load.start()

    def part_of(p):
        return pl.ds(pl.multiple_of(p * sub, PAIR), sub)

    def remote(src, dst, send_sem, recv_sem, dev):
        return pltpu.make_async_remote_copy(
            src_ref=src,
            dst_ref=dst,
            send_sem=send_sem,
            recv_sem=recv_sem,
            device_id={"col": dev},
            device_id_type=MESH,
        )

    def zone_copy(dev):
        return remote(zone_ref, zones.at[me], zsend, zrecv, dev)

    def spread(dev):
        return remote(tile.at[:, part_of(dev - low_home)], slots.at[me], send1, recv1, dev)

    def deliver(dev):
        return remote(stage.at[dev], gold.at[mine], send2, recv2, dev)

    def several(ref, count, send_sem, recv_sem):
        rest = ref.at[pl.ds(0, count)]
        return remote(rest, rest, send_sem, recv_sem, lax.rem(me + 1, n))

    def wait_homes(wait):
        @pl.when(is_home)
        def _():
            wait(half - 1)

        @pl.when(not_home)
        def _():
            wait(half)

    barrier = pltpu.get_barrier_semaphore()

    first_later = jnp.where(is_home, me + 1, jnp.maximum(me + 1, low_home))
    end_later = jnp.where(is_home, n, jnp.maximum(first_later, end_home))

    @pl.loop(first_later, end_later)
    def _(dev):
        pl.semaphore_signal(barrier, inc=1, device_id={"col": dev}, device_id_type=MESH)

    k_copy.start()
    mask_copy.start()
    owner_load.start()
    zone_load.wait()
    tile_copy.wait()

    greetings = jnp.where(is_home, me, jnp.where(me < low_home, 0, half))

    @pl.when(greetings > 0)
    def _():
        pl.semaphore_wait(barrier, greetings)

    @pl.when(is_home)
    def _():
        @pl.loop(0, me)
        def _(dev):
            pl.semaphore_signal(gates.at[block], inc=1, device_id={"col": dev}, device_id_type=MESH)

    def send_to(first, last):
        @pl.loop(first, last)
        def _(dev):
            zone_copy(dev).start()

        @pl.loop(first, last)
        def _(dev):
            spread(dev).start()


    send_to(low_home, jnp.clip(me, low_home, end_home))
    lanes = [slice(t * PAIR, (t + 1) * PAIR) for t in range(W * C // PAIR)]
    t_f = to_pixels([tile[:, at] for at in lanes], rows, pixels).T
    t_ref[...] = t_f
    tb_ref[...] = t_f.astype(jnp.bfloat16)

    @pl.when(is_home)
    def _():
        slots[me] = tile[:, part_of(mine)]

    k_copy.wait()
    for i in range(2):
        for dy in range(3):
            w_ref[i, dy * C : (dy + 1) * C, :] = k_ref[i, :, dy * 3 * C : (dy + 1) * 3 * C]
    mask_copy.wait()
    owner_load.wait()

    for b in range(low_home // BLOCK, end_home // BLOCK):
        first = jnp.maximum(me + 1, b * BLOCK)
        last = (b + 1) * BLOCK

        @pl.when(last > first)
        def _():
            pl.semaphore_wait(gates.at[b], last - first)
            send_to(first, last)

    @pl.when(is_home)
    def _():
        several(zones, n - 1, zsend, zrecv).wait_recv()
        wanted = [lax.rem(me + o, n) for o in range(1, n)]
        wanted = [(dev, owner_ref[zones[dev, 0]]) for dev in wanted]
        several(slots, n - 1, send1, recv1).wait_recv()
        for dev, owner in wanted:
            stage[dev] = slots[owner]
            deliver(dev).start()
        gold[mine] = slots[owner_ref[zone_ref[0]]]

    row = lax.broadcasted_iota(jnp.int32, (8, W), 0)
    column = lax.broadcasted_iota(jnp.int32, (8, W), 1)

    def near(k, b):
        gap = 16 * b + 8 * k + row - column
        return jnp.logical_and(gap >= -8, gap < 8)

    def inside(k, b):
        gap = 16 * b + 8 * k + row - column
        return jnp.logical_and(gap >= -SHIFT, gap <= SHIFT)

    def fold(k, v):
        v = v.reshape(H, 8, 8, W)
        total = jnp.zeros((H, 8, W), jnp.float32)
        for b in range(8):
            total = jnp.where(near(k, b)[None], v[:, b], total)
        return total

    t_b = tb_ref[...]
    gts = []
    squares = []
    wait_homes(lambda count: several(gold, count, send2, recv2).wait_recv())
    for k in range(FOLDS):
        tiles = [(b * FOLDS + k) * (8 // 2) + t for b in range(8) for t in range(8 // 2)]
        places = [(t * PAIR // sub, t * PAIR % sub) for t in tiles]
        g_f = to_pixels([gold[p, :, at : at + PAIR] for p, at in places], rows, pixels)
        g = g_f.astype(jnp.bfloat16)
        gts.append(g_f.T.astype(jnp.bfloat16))
        for y in range(0, H, 2):
            gram = jnp.dot(g, t_b[:, y * W : (y + 2) * W], preferred_element_type=jnp.float32)
            for i in range(2):
                cross[y + i, :, 8 * k : 8 * k + 8, :] = fold(k, gram[:, i * W : (i + 1) * W])
        square = jnp.sum(g_f * g_f, axis=1, keepdims=True)
        squares.append(fold(k, jnp.broadcast_to(square, (H * W // FOLDS, W))))
    gt = jnp.concatenate(gts, axis=1)
    for y in range(H):
        cross[y] = diagonal_box(cross[y]) * SCALE
    other_rows = diagonal_box(jnp.concatenate(squares, axis=1))
    windows = {}

    def other_window(lo, hi):
        lo, hi = max(lo, 0), min(hi, H - 1)
        if (lo, hi) not in windows:
            total = other_rows[lo]
            for r in range(lo + 1, hi + 1):
                total = total + other_rows[r]
            windows[lo, hi] = total
        return windows[lo, hi]

    t_f = t_ref[...]
    own = jnp.sum(t_f * t_f, axis=0, keepdims=True)
    own_rows = [own[:, y * W : (y + 1) * W] for y in range(H)]
    slot = lax.broadcasted_iota(jnp.int32, (16, W), 0)
    shift = lax.rem(slot - lax.broadcasted_iota(jnp.int32, (16, W), 1) + W + 8, 16) - 8
    used = jnp.logical_and(shift >= -SHIFT, shift <= SHIFT)

    def weights_of(y):
        lo_y, hi_y = max(0, y - REACH), min(H - 1, y + REACH)
        self_energy = own_rows[lo_y]
        for r in range(lo_y + 1, hi_y + 1):
            self_energy = self_energy + own_rows[r]
        self_energy = jnp.broadcast_to(lane_box(self_energy), (16, W))
        denom = jnp.zeros((16, W), jnp.float32)
        picked = {}
        for a in range(-SHIFT, SHIFT + 1):
            num = None
            for r in range(lo_y, hi_y + 1):
                if 0 <= r + a < H:
                    num = cross[r, r + a] if num is None else num + cross[r, r + a]
            if num is None:
                denom = denom + 1.0
                continue
            expo = jnp.exp2(num * lax.rsqrt(self_energy * other_window(lo_y + a, hi_y + a) + 1e-05))
            if 0 <= y + a < H:
                picked[y + a] = expo.astype(jnp.bfloat16)
                expo = picked[y + a].astype(jnp.float32)
            denom = denom + expo
        total = jnp.sum(jnp.where(used, denom, 0.0), axis=0, keepdims=True)
        wides = []
        zeros = jnp.zeros((8, W), jnp.float32)
        for k in range(FOLDS):
            for r in range(H):
                value = picked[r].astype(jnp.float32)[8 * k : 8 * k + 8] if r in picked else zeros
                for b in range(8):
                    wides.append(jnp.where(inside(k, b), value, 0.0) if r in picked else zeros)
        return jnp.concatenate(wides, axis=0).astype(jnp.bfloat16), total

    for y in range(0, H, 2):
        pair = [weights_of(y), weights_of(y + 1)]
        wide = jnp.concatenate([p[0] for p in pair], axis=1)
        numer = jnp.dot(gt, wide, preferred_element_type=jnp.float32)
        total = jnp.concatenate([p[1] for p in pair], axis=1)
        cols = slice(y * W, (y + 2) * W)
        res[:, cols] = (t_f[:, cols] - numer / total).astype(jnp.bfloat16).astype(jnp.float32)

    residual = res[...]
    hidden = jnp.maximum(conv_rows(residual, stack, w_ref[0]), 0.0)
    hidden = hidden.astype(jnp.bfloat16).astype(jnp.float32)
    refined = residual + conv_rows(hidden, stack, w_ref[1])
    flat = jnp.sum(refined * refined, axis=0, keepdims=True) * (1.0 / C)
    energy = jnp.concatenate([flat[:, y * W : (y + 1) * W] for y in range(H)], axis=0)
    masked = mask_ref[0].astype(jnp.float32)
    die_sum = jnp.sum(jnp.sum(energy * masked, axis=1, keepdims=True), axis=0, keepdims=True)
    die_count = jnp.sum(jnp.sum(masked, axis=1, keepdims=True), axis=0, keepdims=True)
    lane = lax.broadcasted_iota(jnp.int32, (1, W), 1)
    zone = zone_ref[0]
    at_sum = lane == zone
    at_count = lane == zone + W // 2
    parts[0] = jnp.where(at_sum, die_sum, jnp.where(at_count, die_count, 0.0))

    def give(k):
        return remote(parts.at[0], parts.at[k], part_send, part_recv, lax.rem(me + k, n))

    for k in range(1, n):
        give(k).start()

    wait_homes(lambda count: several(zones, count, zsend, zrecv).wait_send())
    wait_homes(lambda count: several(slots, count, send1, recv1).wait_send())

    @pl.when(is_home)
    def _():
        several(stage, n - 1, send2, recv2).wait_send()

    rest = parts.at[pl.ds(1, n - 1)]
    give_all = remote(rest, rest, part_send, part_recv, lax.rem(me + 1, n))
    give_all.wait_recv()
    total = jnp.sum(parts[...], axis=0)
    zone_sum = jnp.sum(jnp.where(at_sum, total, 0.0), axis=1, keepdims=True)
    zone_count = jnp.sum(jnp.where(at_count, total, 0.0), axis=1, keepdims=True)
    mean = zone_sum / jnp.maximum(zone_count, 1.0)
    score_ref[0] = energy / (mean + 0.01)
    give_all.wait_send()


def body(n, features, zone_ids, golden_owner, defect_mask, kernels):
    half = n // 2
    sub = W * C // half
    vmem = pl.BlockSpec(memory_space=pltpu.VMEM)
    hbm = pl.BlockSpec(memory_space=pl.ANY)
    dma = pltpu.SemaphoreType.DMA
    return pl.pallas_call(
        functools.partial(whole_kernel, n),
        out_shape=jax.ShapeDtypeStruct((1, H, W), jnp.float32),
        in_specs=[hbm] * 5,
        out_specs=vmem,
        scratch_shapes=[
            pltpu.SMEM((1,), jnp.int32),
            pltpu.SMEM(golden_owner.shape, jnp.int32),
            pltpu.VMEM((1, H, W), jnp.int32),
            pltpu.VMEM((H, W * C), jnp.bfloat16),
            pltpu.VMEM((2, C, 9 * C), jnp.bfloat16),
            pltpu.VMEM((2, 3 * C, 3 * C), jnp.bfloat16),
            pltpu.VMEM((n, H, sub), jnp.bfloat16),
            pltpu.VMEM((n, H, sub), jnp.bfloat16),
            pltpu.VMEM((half, H, sub), jnp.bfloat16),
            pltpu.SMEM((n, 1), jnp.int32),
            pltpu.VMEM((H * W * C // 128, 128), jnp.float32),
            pltpu.VMEM((H * W, 128), jnp.float32),
            pltpu.VMEM((C, H * W), jnp.float32),
            pltpu.VMEM((C, H * W), jnp.bfloat16),
            pltpu.VMEM((H, H, 16, W), jnp.float32),
            pltpu.VMEM((C, H * W), jnp.float32),
            pltpu.VMEM((3 * C, H * W), jnp.bfloat16),
            pltpu.VMEM((n, 1, W), jnp.float32),
            pltpu.SemaphoreType.REGULAR((n // BLOCK,)),
            dma((5,)),
            dma,
            dma,
            dma,
            dma,
            dma,
            dma,
            dma,
            dma,
        ],
        compiler_params=pltpu.CompilerParams(collective_id=0, has_side_effects=True),
    )(zone_ids, golden_owner, features, defect_mask, jnp.swapaxes(kernels, 1, 2))


def solution(mesh):
    in_specs = (
        P(("groups", "col"), None, None),
        P(("groups", "col")),
        P("groups"),
        P(("groups", "col"), None, None),
        P(),
    )
    out_specs = P(("groups", "col"), None, None)
    run = functools.partial(body, mesh.shape["col"])
    return jax.shard_map(run, mesh=mesh, in_specs=in_specs, out_specs=out_specs, check_vma=False)
```

```python
import functools
import math

import jax
import jax.numpy as jnp
from jax import lax
from jax.experimental import pallas as pl
from jax.experimental.pallas import tpu as pltpu
from jax.sharding import PartitionSpec as P

C = 64
H = 8
W = 128
SHIFT = 6
REACH = 2
FOLDS = 2
BLOCK = 4
PAIR = 2 * C
SCALE = 32.0 * math.log2(math.e)
MESH = pl.DeviceIdType.MESH


def lane_box(v):
    lane = lax.broadcasted_iota(jnp.int32, v.shape, v.ndim - 1)
    total = v
    for d in range(1, REACH + 1):
        right = pltpu.roll(v, d, v.ndim - 1)
        left = pltpu.roll(v, W - d, v.ndim - 1)
        total = total + jnp.where(lane >= d, right, 0.0) + jnp.where(lane < W - d, left, 0.0)
    return total


def diagonal_box(v):
    lane = lax.broadcasted_iota(jnp.int32, v.shape, v.ndim - 1)
    total = v
    for d in range(1, REACH + 1):
        back = pltpu.roll(pltpu.roll(v, d, v.ndim - 1), d, v.ndim - 2)
        ahead = pltpu.roll(pltpu.roll(v, W - d, v.ndim - 1), 16 - d, v.ndim - 2)
        total = total + jnp.where(lane >= d, back, 0.0) + jnp.where(lane < W - d, ahead, 0.0)
    return total


def conv_rows(tile_f, views, weights):
    lane = lax.rem(lax.broadcasted_iota(jnp.int32, (C, H * W), 1), W)
    pixels = H * W
    views[0:C, :] = jnp.where(lane >= 1, pltpu.roll(tile_f, 1, 1), 0.0).astype(jnp.bfloat16)
    views[C : 2 * C, :] = tile_f.astype(jnp.bfloat16)
    right = jnp.where(lane < W - 1, pltpu.roll(tile_f, pixels - 1, 1), 0.0)
    views[2 * C : 3 * C, :] = right.astype(jnp.bfloat16)
    sums = jnp.dot(weights, views[...], preferred_element_type=jnp.float32)
    zeros = jnp.zeros((C, W), jnp.float32)
    above = jnp.concatenate([zeros, sums[0:C, 0 : pixels - W]], axis=1)
    below = jnp.concatenate([sums[2 * C : 3 * C, W:pixels], zeros], axis=1)
    return above + sums[C : 2 * C] + below


def to_pixels(tiles, rows, pixels):
    for at, tile in enumerate(tiles):
        rows[at * H : (at + 1) * H, :] = tile.astype(jnp.float32)
    pairs = len(tiles)
    for y in range(H):
        v = rows[pl.ds(y, pairs, stride=H), :]
        pixels[pl.ds(y * 2 * pairs, pairs, stride=2), :] = v
        pixels[pl.ds(y * 2 * pairs + 1, pairs, stride=2), :] = pltpu.roll(v, C, 1)
    return pixels[0 : H * 2 * pairs, 0:C]


def whole_kernel(
    n,
    zone_hbm, owner_hbm, feat_ref, mask_hbm, k_hbm, score_ref,
    zone_ref, owner_ref, mask_ref, tile, k_ref, w_ref, slots, stage, gold, zones,
    rows, pixels, t_ref, tb_ref, cross, res, stack, parts,
    gates, local, send1, recv1, send2, recv2, zsend, zrecv, part_send, part_recv,
):
    half = n // 2
    low_home, end_home = n // 4, n // 4 + half
    sub = W * C // half
    me = lax.axis_index("col")
    block = me // BLOCK
    is_home = jnp.logical_and(me >= low_home, me < end_home)
    not_home = jnp.logical_not(is_home)
    mine = me - low_home

    tile_copy = pltpu.make_async_copy(feat_ref.at[0], tile, local.at[0])
    k_copy = pltpu.make_async_copy(k_hbm, k_ref, local.at[1])
    mask_copy = pltpu.make_async_copy(mask_hbm, mask_ref, local.at[2])
    zone_load = pltpu.make_async_copy(zone_hbm, zone_ref, local.at[3])
    owner_load = pltpu.make_async_copy(owner_hbm, owner_ref, local.at[4])
    tile_copy.start()
    zone_load.start()

    def part_of(p):
        return pl.ds(pl.multiple_of(p * sub, PAIR), sub)

    def remote(src, dst, send_sem, recv_sem, dev):
        return pltpu.make_async_remote_copy(
            src_ref=src,
            dst_ref=dst,
            send_sem=send_sem,
            recv_sem=recv_sem,
            device_id={"col": dev},
            device_id_type=MESH,
        )

    def zone_copy(dev):
        return remote(zone_ref, zones.at[me], zsend, zrecv, dev)

    def spread(dev):
        return remote(tile.at[:, part_of(dev - low_home)], slots.at[me], send1, recv1, dev)

    def deliver(dev):
        return remote(stage.at[dev], gold.at[mine], send2, recv2, dev)

    def several(ref, count, send_sem, recv_sem):
        rest = ref.at[pl.ds(0, count)]
        return remote(rest, rest, send_sem, recv_sem, lax.rem(me + 1, n))

    def wait_homes(wait):
        @pl.when(is_home)
        def _():
            wait(half - 1)

        @pl.when(not_home)
        def _():
            wait(half)

    barrier = pltpu.get_barrier_semaphore()

    first_later = jnp.where(is_home, me + 1, jnp.maximum(me + 1, low_home))
    end_later = jnp.where(is_home, n, jnp.maximum(first_later, end_home))

    @pl.loop(first_later, end_later)
    def _(dev):
        pl.semaphore_signal(barrier, inc=1, device_id={"col": dev}, device_id_type=MESH)

    k_copy.start()
    mask_copy.start()
    owner_load.start()
    zone_load.wait()
    tile_copy.wait()

    greetings = jnp.where(is_home, me, jnp.where(me < low_home, 0, half))

    @pl.when(greetings > 0)
    def _():
        pl.semaphore_wait(barrier, greetings)

    @pl.when(is_home)
    def _():
        @pl.loop(0, me)
        def _(dev):
            pl.semaphore_signal(gates.at[block], inc=1, device_id={"col": dev}, device_id_type=MESH)

    def send_to(first, last):
        @pl.loop(first, last)
        def _(dev):
            zone_copy(dev).start()

        @pl.loop(first, last)
        def _(dev):
            spread(dev).start()


    send_to(low_home, jnp.clip(me, low_home, end_home))
    lanes = [slice(t * PAIR, (t + 1) * PAIR) for t in range(W * C // PAIR)]
    t_f = to_pixels([tile[:, at] for at in lanes], rows, pixels).T
    t_ref[...] = t_f
    tb_ref[...] = t_f.astype(jnp.bfloat16)

    @pl.when(is_home)
    def _():
        slots[me] = tile[:, part_of(mine)]

    k_copy.wait()
    for i in range(2):
        for dy in range(3):
            w_ref[i, dy * C : (dy + 1) * C, :] = k_ref[i, :, dy * 3 * C : (dy + 1) * 3 * C]
    mask_copy.wait()
    owner_load.wait()

    for b in range(low_home // BLOCK, end_home // BLOCK):
        first = jnp.maximum(me + 1, b * BLOCK)
        last = (b + 1) * BLOCK

        @pl.when(last > first)
        def _():
            pl.semaphore_wait(gates.at[b], last - first)
            send_to(first, last)

    @pl.when(is_home)
    def _():
        several(zones, n - 1, zsend, zrecv).wait_recv()
        wanted = [lax.rem(me + o, n) for o in range(1, n)]
        wanted = [(dev, owner_ref[zones[dev, 0]]) for dev in wanted]
        several(slots, n - 1, send1, recv1).wait_recv()
        for dev, owner in wanted:
            stage[dev] = slots[owner]
            deliver(dev).start()
        gold[mine] = slots[owner_ref[zone_ref[0]]]

    row = lax.broadcasted_iota(jnp.int32, (8, W), 0)
    column = lax.broadcasted_iota(jnp.int32, (8, W), 1)

    def near(k, b):
        gap = 16 * b + 8 * k + row - column
        return jnp.logical_and(gap >= -8, gap < 8)

    def inside(k, b):
        gap = 16 * b + 8 * k + row - column
        return jnp.logical_and(gap >= -SHIFT, gap <= SHIFT)

    def fold(k, v):
        v = v.reshape(H, 8, 8, W)
        total = jnp.zeros((H, 8, W), jnp.float32)
        for b in range(8):
            total = jnp.where(near(k, b)[None], v[:, b], total)
        return total

    t_b = tb_ref[...]
    gts = []
    squares = []
    wait_homes(lambda count: several(gold, count, send2, recv2).wait_recv())
    for k in range(FOLDS):
        tiles = [(b * FOLDS + k) * (8 // 2) + t for b in range(8) for t in range(8 // 2)]
        places = [(t * PAIR // sub, t * PAIR % sub) for t in tiles]
        g_f = to_pixels([gold[p, :, at : at + PAIR] for p, at in places], rows, pixels)
        g = g_f.astype(jnp.bfloat16)
        gts.append(g_f.T.astype(jnp.bfloat16))
        for y in range(0, H, 2):
            gram = jnp.dot(g, t_b[:, y * W : (y + 2) * W], preferred_element_type=jnp.float32)
            for i in range(2):
                cross[y + i, :, 8 * k : 8 * k + 8, :] = fold(k, gram[:, i * W : (i + 1) * W])
        square = jnp.sum(g_f * g_f, axis=1, keepdims=True)
        squares.append(fold(k, jnp.broadcast_to(square, (H * W // FOLDS, W))))
    gt = jnp.concatenate(gts, axis=1)
    for y in range(H):
        cross[y] = diagonal_box(cross[y]) * SCALE
    other_rows = diagonal_box(jnp.concatenate(squares, axis=1))
    windows = {}

    def other_window(lo, hi):
        lo, hi = max(lo, 0), min(hi, H - 1)
        if (lo, hi) not in windows:
            total = other_rows[lo]
            for r in range(lo + 1, hi + 1):
                total = total + other_rows[r]
            windows[lo, hi] = total
        return windows[lo, hi]

    t_f = t_ref[...]
    own = jnp.sum(t_f * t_f, axis=0, keepdims=True)
    own_rows = [own[:, y * W : (y + 1) * W] for y in range(H)]
    slot = lax.broadcasted_iota(jnp.int32, (16, W), 0)
    shift = lax.rem(slot - lax.broadcasted_iota(jnp.int32, (16, W), 1) + W + 8, 16) - 8
    used = jnp.logical_and(shift >= -SHIFT, shift <= SHIFT)

    def weights_of(y):
        lo_y, hi_y = max(0, y - REACH), min(H - 1, y + REACH)
        self_energy = own_rows[lo_y]
        for r in range(lo_y + 1, hi_y + 1):
            self_energy = self_energy + own_rows[r]
        self_energy = jnp.broadcast_to(lane_box(self_energy), (16, W))
        denom = jnp.zeros((16, W), jnp.float32)
        picked = {}
        for a in range(-SHIFT, SHIFT + 1):
            num = None
            for r in range(lo_y, hi_y + 1):
                if 0 <= r + a < H:
                    num = cross[r, r + a] if num is None else num + cross[r, r + a]
            if num is None:
                denom = denom + 1.0
                continue
            expo = jnp.exp2(num * lax.rsqrt(self_energy * other_window(lo_y + a, hi_y + a) + 1e-05))
            if 0 <= y + a < H:
                picked[y + a] = expo.astype(jnp.bfloat16)
                expo = picked[y + a].astype(jnp.float32)
            denom = denom + expo
        total = jnp.sum(jnp.where(used, denom, 0.0), axis=0, keepdims=True)
        wides = []
        zeros = jnp.zeros((8, W), jnp.float32)
        for k in range(FOLDS):
            for r in range(H):
                value = picked[r].astype(jnp.float32)[8 * k : 8 * k + 8] if r in picked else zeros
                for b in range(8):
                    wides.append(jnp.where(inside(k, b), value, 0.0) if r in picked else zeros)
        return jnp.concatenate(wides, axis=0).astype(jnp.bfloat16), total

    for y in range(0, H, 2):
        pair = [weights_of(y), weights_of(y + 1)]
        wide = jnp.concatenate([p[0] for p in pair], axis=1)
        numer = jnp.dot(gt, wide, preferred_element_type=jnp.float32)
        total = jnp.concatenate([p[1] for p in pair], axis=1)
        cols = slice(y * W, (y + 2) * W)
        res[:, cols] = (t_f[:, cols] - numer / total).astype(jnp.bfloat16).astype(jnp.float32)

    residual = res[...]
    hidden = jnp.maximum(conv_rows(residual, stack, w_ref[0]), 0.0)
    hidden = hidden.astype(jnp.bfloat16).astype(jnp.float32)
    refined = residual + conv_rows(hidden, stack, w_ref[1])
    flat = jnp.sum(refined * refined, axis=0, keepdims=True) * (1.0 / C)
    energy = jnp.concatenate([flat[:, y * W : (y + 1) * W] for y in range(H)], axis=0)
    masked = mask_ref[0].astype(jnp.float32)
    die_sum = jnp.sum(jnp.sum(energy * masked, axis=1, keepdims=True), axis=0, keepdims=True)
    die_count = jnp.sum(jnp.sum(masked, axis=1, keepdims=True), axis=0, keepdims=True)
    lane = lax.broadcasted_iota(jnp.int32, (1, W), 1)
    zone = zone_ref[0]
    at_sum = lane == zone
    at_count = lane == zone + W // 2
    parts[0] = jnp.where(at_sum, die_sum, jnp.where(at_count, die_count, 0.0))

    def give(k):
        return remote(parts.at[0], parts.at[k], part_send, part_recv, lax.rem(me + k, n))

    for k in range(1, n):
        give(k).start()

    wait_homes(lambda count: several(zones, count, zsend, zrecv).wait_send())
    wait_homes(lambda count: several(slots, count, send1, recv1).wait_send())

    @pl.when(is_home)
    def _():
        several(stage, n - 1, send2, recv2).wait_send()

    rest = parts.at[pl.ds(1, n - 1)]
    give_all = remote(rest, rest, part_send, part_recv, lax.rem(me + 1, n))
    give_all.wait_recv()
    total = jnp.sum(parts[...], axis=0)
    zone_sum = jnp.sum(jnp.where(at_sum, total, 0.0), axis=1, keepdims=True)
    zone_count = jnp.sum(jnp.where(at_count, total, 0.0), axis=1, keepdims=True)
    mean = zone_sum / jnp.maximum(zone_count, 1.0)
    score_ref[0] = energy / (mean + 0.01)
    give_all.wait_send()


def body(n, features, zone_ids, golden_owner, defect_mask, kernels):
    half = n // 2
    sub = W * C // half
    vmem = pl.BlockSpec(memory_space=pltpu.VMEM)
    hbm = pl.BlockSpec(memory_space=pl.ANY)
    dma = pltpu.SemaphoreType.DMA
    return pl.pallas_call(
        functools.partial(whole_kernel, n),
        out_shape=jax.ShapeDtypeStruct((1, H, W), jnp.float32),
        in_specs=[hbm] * 5,
        out_specs=vmem,
        scratch_shapes=[
            pltpu.SMEM((1,), jnp.int32),
            pltpu.SMEM(golden_owner.shape, jnp.int32),
            pltpu.VMEM((1, H, W), jnp.int32),
            pltpu.VMEM((H, W * C), jnp.bfloat16),
            pltpu.VMEM((2, C, 9 * C), jnp.bfloat16),
            pltpu.VMEM((2, 3 * C, 3 * C), jnp.bfloat16),
            pltpu.VMEM((n, H, sub), jnp.bfloat16),
            pltpu.VMEM((n, H, sub), jnp.bfloat16),
            pltpu.VMEM((half, H, sub), jnp.bfloat16),
            pltpu.SMEM((n, 1), jnp.int32),
            pltpu.VMEM((H * W * C // 128, 128), jnp.float32),
            pltpu.VMEM((H * W, 128), jnp.float32),
            pltpu.VMEM((C, H * W), jnp.float32),
            pltpu.VMEM((C, H * W), jnp.bfloat16),
            pltpu.VMEM((H, H, 16, W), jnp.float32),
            pltpu.VMEM((C, H * W), jnp.float32),
            pltpu.VMEM((3 * C, H * W), jnp.bfloat16),
            pltpu.VMEM((n, 1, W), jnp.float32),
            pltpu.SemaphoreType.REGULAR((n // BLOCK,)),
            dma((5,)),
            dma,
            dma,
            dma,
            dma,
            dma,
            dma,
            dma,
            dma,
        ],
        compiler_params=pltpu.CompilerParams(collective_id=0, has_side_effects=True, vmem_limit_bytes=24 * 1024 * 1024
        ),
    )(zone_ids, *[pltpu.with_memory_space_constraint(v, pltpu.HBM) for v in (golden_owner, features, defect_mask, jnp.swapaxes(kernels, 1, 2))])


def solution(mesh):
    in_specs = (
        P(("groups", "col"), None, None),
        P(("groups", "col")),
        P("groups"),
        P(("groups", "col"), None, None),
        P(),
    )
    out_specs = P(("groups", "col"), None, None)
    run = functools.partial(body, mesh.shape["col"])
    return jax.shard_map(run, mesh=mesh, in_specs=in_specs, out_specs=out_specs, check_vma=False)
```

```python
import functools
import math

import jax
import jax.numpy as jnp
from jax import lax
from jax.experimental import pallas as pl
from jax.experimental.pallas import tpu as pltpu
from jax.sharding import PartitionSpec as P

C = 64
H = 8
W = 128
SHIFT = 6
REACH = 2
FOLDS = 2
BLOCK = 4
PAIR = 2 * C
SCALE = 32.0 * math.log2(math.e)
MESH = pl.DeviceIdType.MESH


def lane_box(v):
    lane = lax.broadcasted_iota(jnp.int32, v.shape, v.ndim - 1)
    total = v
    for d in range(1, REACH + 1):
        right = pltpu.roll(v, d, v.ndim - 1)
        left = pltpu.roll(v, W - d, v.ndim - 1)
        total = total + jnp.where(lane >= d, right, 0.0) + jnp.where(lane < W - d, left, 0.0)
    return total


def diagonal_box(v):
    lane = lax.broadcasted_iota(jnp.int32, v.shape, v.ndim - 1)
    total = v
    for d in range(1, REACH + 1):
        back = pltpu.roll(pltpu.roll(v, d, v.ndim - 1), d, v.ndim - 2)
        ahead = pltpu.roll(pltpu.roll(v, W - d, v.ndim - 1), 16 - d, v.ndim - 2)
        total = total + jnp.where(lane >= d, back, 0.0) + jnp.where(lane < W - d, ahead, 0.0)
    return total


def conv_rows(tile_f, views, weights):
    lane = lax.rem(lax.broadcasted_iota(jnp.int32, (C, H * W), 1), W)
    pixels = H * W
    views[0:C, :] = jnp.where(lane >= 1, pltpu.roll(tile_f, 1, 1), 0.0).astype(jnp.bfloat16)
    views[C : 2 * C, :] = tile_f.astype(jnp.bfloat16)
    right = jnp.where(lane < W - 1, pltpu.roll(tile_f, pixels - 1, 1), 0.0)
    views[2 * C : 3 * C, :] = right.astype(jnp.bfloat16)
    sums = jnp.dot(weights, views[...], preferred_element_type=jnp.float32)
    zeros = jnp.zeros((C, W), jnp.float32)
    above = jnp.concatenate([zeros, sums[0:C, 0 : pixels - W]], axis=1)
    below = jnp.concatenate([sums[2 * C : 3 * C, W:pixels], zeros], axis=1)
    return above + sums[C : 2 * C] + below


def to_pixels(tiles, rows, pixels):
    for at, tile in enumerate(tiles):
        rows[at * H : (at + 1) * H, :] = tile.astype(jnp.float32)
    pairs = len(tiles)
    for y in range(H):
        v = rows[pl.ds(y, pairs, stride=H), :]
        pixels[pl.ds(y * 2 * pairs, pairs, stride=2), :] = v
        pixels[pl.ds(y * 2 * pairs + 1, pairs, stride=2), :] = pltpu.roll(v, C, 1)
    return pixels[0 : H * 2 * pairs, 0:C]


def whole_kernel(
    n,
    zone_ref, owner_hbm, feat_ref, mask_hbm, k_hbm, score_ref,
    owner_ref, mask_ref, tile, k_ref, w_ref, slots, stage, gold, zones,
    rows, pixels, t_ref, tb_ref, cross, res, stack, parts,
    gates, local, send1, recv1, send2, recv2, zsend, zrecv, part_send, part_recv,
):
    half = n // 2
    low_home, end_home = n // 4, n // 4 + half
    sub = W * C // half
    me = lax.axis_index("col")
    block = me // BLOCK
    is_home = jnp.logical_and(me >= low_home, me < end_home)
    not_home = jnp.logical_not(is_home)
    mine = me - low_home

    tile_copy = pltpu.make_async_copy(feat_ref.at[0], tile, local.at[0])
    k_copy = pltpu.make_async_copy(k_hbm, k_ref, local.at[1])
    mask_copy = pltpu.make_async_copy(mask_hbm, mask_ref, local.at[2])
    owner_load = pltpu.make_async_copy(owner_hbm, owner_ref, local.at[3])
    tile_copy.start()

    def part_of(p):
        return pl.ds(pl.multiple_of(p * sub, PAIR), sub)

    def remote(src, dst, send_sem, recv_sem, dev):
        return pltpu.make_async_remote_copy(
            src_ref=src,
            dst_ref=dst,
            send_sem=send_sem,
            recv_sem=recv_sem,
            device_id={"col": dev},
            device_id_type=MESH,
        )

    def zone_copy(dev):
        return remote(zone_ref, zones.at[me], zsend, zrecv, dev)

    def spread(dev):
        return remote(tile.at[:, part_of(dev - low_home)], slots.at[me], send1, recv1, dev)

    def deliver(dev):
        return remote(stage.at[dev], gold.at[mine], send2, recv2, dev)

    def several(ref, count, send_sem, recv_sem):
        rest = ref.at[pl.ds(0, count)]
        return remote(rest, rest, send_sem, recv_sem, lax.rem(me + 1, n))

    def wait_homes(wait):
        @pl.when(is_home)
        def _():
            wait(half - 1)

        @pl.when(not_home)
        def _():
            wait(half)

    barrier = pltpu.get_barrier_semaphore()

    first_later = jnp.where(is_home, me + 1, jnp.maximum(me + 1, low_home))
    end_later = jnp.where(is_home, n, jnp.maximum(first_later, end_home))

    @pl.loop(first_later, end_later)
    def _(dev):
        pl.semaphore_signal(barrier, inc=1, device_id={"col": dev}, device_id_type=MESH)

    k_copy.start()
    mask_copy.start()
    owner_load.start()

    greetings = jnp.where(is_home, me, jnp.where(me < low_home, 0, half))

    @pl.when(greetings > 0)
    def _():
        pl.semaphore_wait(barrier, greetings)

    @pl.when(is_home)
    def _():
        @pl.loop(0, me)
        def _(dev):
            pl.semaphore_signal(gates.at[block], inc=1, device_id={"col": dev}, device_id_type=MESH)

    def send_to(first, last):
        @pl.loop(first, last)
        def _(dev):
            zone_copy(dev).start()

        @pl.loop(first, last)
        def _(dev):
            spread(dev).start()


    tile_copy.wait()
    send_to(low_home, jnp.clip(me, low_home, end_home))
    lanes = [slice(t * PAIR, (t + 1) * PAIR) for t in range(W * C // PAIR)]
    t_f = to_pixels([tile[:, at] for at in lanes], rows, pixels).T
    t_ref[...] = t_f
    tb_ref[...] = t_f.astype(jnp.bfloat16)

    @pl.when(is_home)
    def _():
        slots[me] = tile[:, part_of(mine)]

    k_copy.wait()
    for i in range(2):
        for dy in range(3):
            w_ref[i, dy * C : (dy + 1) * C, :] = k_ref[i, :, dy * 3 * C : (dy + 1) * 3 * C]
    mask_copy.wait()
    owner_load.wait()

    for b in range(low_home // BLOCK, end_home // BLOCK):
        first = jnp.maximum(me + 1, b * BLOCK)
        last = (b + 1) * BLOCK

        @pl.when(last > first)
        def _():
            pl.semaphore_wait(gates.at[b], last - first)
            send_to(first, last)

    @pl.when(is_home)
    def _():
        several(zones, n - 1, zsend, zrecv).wait_recv()
        upper = me // half
        quarter = low_home
        flips = [*range(n - 1, half - 1, -1), *range(quarter)]
        wanted = [c + upper * (n - 1 - 2 * c) for c in flips]
        first_mate = quarter + upper * quarter
        at = me - first_mate
        wanted += [first_mate + lax.rem(at + o, quarter) for o in range(1, quarter)]
        wanted = [(dev, owner_ref[zones[dev, 0]]) for dev in wanted]
        several(slots, n - 1, send1, recv1).wait_recv()
        for dev, owner in wanted:
            stage[dev] = slots[owner]
            deliver(dev).start()
        gold[mine] = slots[owner_ref[zone_ref[0]]]

    row = lax.broadcasted_iota(jnp.int32, (8, W), 0)
    column = lax.broadcasted_iota(jnp.int32, (8, W), 1)

    def near(k, b):
        gap = 16 * b + 8 * k + row - column
        return jnp.logical_and(gap >= -8, gap < 8)

    def inside(k, b):
        gap = 16 * b + 8 * k + row - column
        return jnp.logical_and(gap >= -SHIFT, gap <= SHIFT)

    def fold(k, v):
        v = v.reshape(H, 8, 8, W)
        total = jnp.zeros((H, 8, W), jnp.float32)
        for b in range(8):
            total = jnp.where(near(k, b)[None], v[:, b], total)
        return total

    t_b = tb_ref[...]
    gts = []
    squares = []
    wait_homes(lambda count: several(gold, count, send2, recv2).wait_recv())
    for k in range(FOLDS):
        tiles = [(b * FOLDS + k) * (8 // 2) + t for b in range(8) for t in range(8 // 2)]
        places = [(t * PAIR // sub, t * PAIR % sub) for t in tiles]
        g_f = to_pixels([gold[p, :, at : at + PAIR] for p, at in places], rows, pixels)
        g = g_f.astype(jnp.bfloat16)
        gts.append(g_f.T.astype(jnp.bfloat16))
        for y in range(0, H, 2):
            gram = jnp.dot(g, t_b[:, y * W : (y + 2) * W], preferred_element_type=jnp.float32)
            for i in range(2):
                cross[y + i, :, 8 * k : 8 * k + 8, :] = fold(k, gram[:, i * W : (i + 1) * W])
        square = jnp.sum(g_f * g_f, axis=1, keepdims=True)
        squares.append(fold(k, jnp.broadcast_to(square, (H * W // FOLDS, W))))
    gt = jnp.concatenate(gts, axis=1)
    for y in range(H):
        cross[y] = diagonal_box(cross[y]) * SCALE
    other_rows = diagonal_box(jnp.concatenate(squares, axis=1))
    windows = {}

    def other_window(lo, hi):
        lo, hi = max(lo, 0), min(hi, H - 1)
        if (lo, hi) not in windows:
            total = other_rows[lo]
            for r in range(lo + 1, hi + 1):
                total = total + other_rows[r]
            windows[lo, hi] = total
        return windows[lo, hi]

    t_f = t_ref[...]
    own = jnp.sum(t_f * t_f, axis=0, keepdims=True)
    own_rows = [own[:, y * W : (y + 1) * W] for y in range(H)]
    slot = lax.broadcasted_iota(jnp.int32, (16, W), 0)
    shift = lax.rem(slot - lax.broadcasted_iota(jnp.int32, (16, W), 1) + W + 8, 16) - 8
    used = jnp.logical_and(shift >= -SHIFT, shift <= SHIFT)

    def weights_of(y):
        lo_y, hi_y = max(0, y - REACH), min(H - 1, y + REACH)
        self_energy = own_rows[lo_y]
        for r in range(lo_y + 1, hi_y + 1):
            self_energy = self_energy + own_rows[r]
        self_energy = jnp.broadcast_to(lane_box(self_energy), (16, W))
        denom = jnp.zeros((16, W), jnp.float32)
        picked = {}
        for a in range(-SHIFT, SHIFT + 1):
            num = None
            for r in range(lo_y, hi_y + 1):
                if 0 <= r + a < H:
                    num = cross[r, r + a] if num is None else num + cross[r, r + a]
            if num is None:
                denom = denom + 1.0
                continue
            expo = jnp.exp2(num * lax.rsqrt(self_energy * other_window(lo_y + a, hi_y + a) + 1e-05))
            if 0 <= y + a < H:
                picked[y + a] = expo.astype(jnp.bfloat16)
                expo = picked[y + a].astype(jnp.float32)
            denom = denom + expo
        total = jnp.sum(jnp.where(used, denom, 0.0), axis=0, keepdims=True)
        wides = []
        zeros = jnp.zeros((8, W), jnp.float32)
        for k in range(FOLDS):
            for r in range(H):
                value = picked[r].astype(jnp.float32)[8 * k : 8 * k + 8] if r in picked else zeros
                for b in range(8):
                    wides.append(jnp.where(inside(k, b), value, 0.0) if r in picked else zeros)
        return jnp.concatenate(wides, axis=0).astype(jnp.bfloat16), total

    for y in range(0, H, 2):
        pair = [weights_of(y), weights_of(y + 1)]
        wide = jnp.concatenate([p[0] for p in pair], axis=1)
        numer = jnp.dot(gt, wide, preferred_element_type=jnp.float32)
        total = jnp.concatenate([p[1] for p in pair], axis=1)
        cols = slice(y * W, (y + 2) * W)
        res[:, cols] = (t_f[:, cols] - numer / total).astype(jnp.bfloat16).astype(jnp.float32)

    residual = res[...]
    hidden = jnp.maximum(conv_rows(residual, stack, w_ref[0]), 0.0)
    hidden = hidden.astype(jnp.bfloat16).astype(jnp.float32)
    refined = residual + conv_rows(hidden, stack, w_ref[1])
    flat = jnp.sum(refined * refined, axis=0, keepdims=True) * (1.0 / C)
    energy = jnp.concatenate([flat[:, y * W : (y + 1) * W] for y in range(H)], axis=0)
    masked = mask_ref[0].astype(jnp.float32)
    die_sum = jnp.sum(jnp.sum(energy * masked, axis=1, keepdims=True), axis=0, keepdims=True)
    die_count = jnp.sum(jnp.sum(masked, axis=1, keepdims=True), axis=0, keepdims=True)
    lane = lax.broadcasted_iota(jnp.int32, (1, W), 1)
    zone = zone_ref[0]
    at_sum = lane == zone
    at_count = lane == zone + W // 2
    parts[0] = jnp.where(at_sum, die_sum, jnp.where(at_count, die_count, 0.0))

    def give(k):
        return remote(parts.at[0], parts.at[k], part_send, part_recv, lax.rem(me + k, n))

    for k in range(1, n):
        give(k).start()

    wait_homes(lambda count: several(zones, count, zsend, zrecv).wait_send())
    wait_homes(lambda count: several(slots, count, send1, recv1).wait_send())

    @pl.when(is_home)
    def _():
        several(stage, n - 1, send2, recv2).wait_send()

    rest = parts.at[pl.ds(1, n - 1)]
    give_all = remote(rest, rest, part_send, part_recv, lax.rem(me + 1, n))
    give_all.wait_recv()
    total = jnp.sum(parts[...], axis=0)
    zone_sum = jnp.sum(jnp.where(at_sum, total, 0.0), axis=1, keepdims=True)
    zone_count = jnp.sum(jnp.where(at_count, total, 0.0), axis=1, keepdims=True)
    mean = zone_sum / jnp.maximum(zone_count, 1.0)
    score_ref[0] = energy / (mean + 0.01)
    give_all.wait_send()


def body(n, features, zone_ids, golden_owner, defect_mask, kernels):
    half = n // 2
    sub = W * C // half
    vmem = pl.BlockSpec(memory_space=pltpu.VMEM)
    hbm = pl.BlockSpec(memory_space=pl.ANY)
    dma = pltpu.SemaphoreType.DMA
    return pl.pallas_call(
        functools.partial(whole_kernel, n),
        out_shape=jax.ShapeDtypeStruct((1, H, W), jnp.float32),
        in_specs=[pl.BlockSpec(memory_space=pltpu.SMEM), hbm, hbm, hbm, hbm],
        out_specs=vmem,
        scratch_shapes=[
            pltpu.SMEM(golden_owner.shape, jnp.int32),
            pltpu.VMEM((1, H, W), jnp.int32),
            pltpu.VMEM((H, W * C), jnp.bfloat16),
            pltpu.VMEM((2, C, 9 * C), jnp.bfloat16),
            pltpu.VMEM((2, 3 * C, 3 * C), jnp.bfloat16),
            pltpu.VMEM((n, H, sub), jnp.bfloat16),
            pltpu.VMEM((n, H, sub), jnp.bfloat16),
            pltpu.VMEM((half, H, sub), jnp.bfloat16),
            pltpu.SMEM((n, 1), jnp.int32),
            pltpu.VMEM((H * W * C // 128, 128), jnp.float32),
            pltpu.VMEM((H * W, 128), jnp.float32),
            pltpu.VMEM((C, H * W), jnp.float32),
            pltpu.VMEM((C, H * W), jnp.bfloat16),
            pltpu.VMEM((H, H, 16, W), jnp.float32),
            pltpu.VMEM((C, H * W), jnp.float32),
            pltpu.VMEM((3 * C, H * W), jnp.bfloat16),
            pltpu.VMEM((n, 1, W), jnp.float32),
            pltpu.SemaphoreType.REGULAR((n // BLOCK,)),
            dma((4,)),
            dma,
            dma,
            dma,
            dma,
            dma,
            dma,
            dma,
            dma,
        ],
        compiler_params=pltpu.CompilerParams(collective_id=0, has_side_effects=True, vmem_limit_bytes=24 * 1024 * 1024
        ),
    )(zone_ids, *[pltpu.with_memory_space_constraint(v, pltpu.HBM) for v in (golden_owner, features, defect_mask, jnp.swapaxes(kernels, 1, 2))])


def solution(mesh):
    in_specs = (
        P(("groups", "col"), None, None),
        P(("groups", "col")),
        P("groups"),
        P(("groups", "col"), None, None),
        P(),
    )
    out_specs = P(("groups", "col"), None, None)
    run = functools.partial(body, mesh.shape["col"])
    return jax.shard_map(run, mesh=mesh, in_specs=in_specs, out_specs=out_specs, check_vma=False)
```

```python
import functools
import math

import jax
import jax.numpy as jnp
from jax import lax
from jax.experimental import pallas as pl
from jax.experimental.pallas import tpu as pltpu
from jax.sharding import PartitionSpec as P

C = 64
H = 8
W = 128
SHIFT = 6
REACH = 2
FOLDS = 2
BLOCK = 4
PAIR = 2 * C
SCALE = 32.0 * math.log2(math.e)
MESH = pl.DeviceIdType.MESH


def lane_box(v):
    lane = lax.broadcasted_iota(jnp.int32, v.shape, v.ndim - 1)
    total = v
    for d in range(1, REACH + 1):
        right = pltpu.roll(v, d, v.ndim - 1)
        left = pltpu.roll(v, W - d, v.ndim - 1)
        total = total + jnp.where(lane >= d, right, 0.0) + jnp.where(lane < W - d, left, 0.0)
    return total


def diagonal_box(v):
    lane = lax.broadcasted_iota(jnp.int32, v.shape, v.ndim - 1)
    total = v
    for d in range(1, REACH + 1):
        back = pltpu.roll(pltpu.roll(v, d, v.ndim - 1), d, v.ndim - 2)
        ahead = pltpu.roll(pltpu.roll(v, W - d, v.ndim - 1), 16 - d, v.ndim - 2)
        total = total + jnp.where(lane >= d, back, 0.0) + jnp.where(lane < W - d, ahead, 0.0)
    return total


def conv_rows(tile_f, views, weights):
    lane = lax.rem(lax.broadcasted_iota(jnp.int32, (C, H * W), 1), W)
    pixels = H * W
    views[0:C, :] = jnp.where(lane >= 1, pltpu.roll(tile_f, 1, 1), 0.0).astype(jnp.bfloat16)
    views[C : 2 * C, :] = tile_f.astype(jnp.bfloat16)
    right = jnp.where(lane < W - 1, pltpu.roll(tile_f, pixels - 1, 1), 0.0)
    views[2 * C : 3 * C, :] = right.astype(jnp.bfloat16)
    sums = jnp.dot(weights, views[...], preferred_element_type=jnp.float32)
    zeros = jnp.zeros((C, W), jnp.float32)
    above = jnp.concatenate([zeros, sums[0:C, 0 : pixels - W]], axis=1)
    below = jnp.concatenate([sums[2 * C : 3 * C, W:pixels], zeros], axis=1)
    return above + sums[C : 2 * C] + below


def to_pixels(tiles, rows, pixels):
    for at, tile in enumerate(tiles):
        rows[at * H : (at + 1) * H, :] = tile.astype(jnp.float32)
    pairs = len(tiles)
    for y in range(H):
        v = rows[pl.ds(y, pairs, stride=H), :]
        pixels[pl.ds(y * 2 * pairs, pairs, stride=2), :] = v
        pixels[pl.ds(y * 2 * pairs + 1, pairs, stride=2), :] = pltpu.roll(v, C, 1)
    return pixels[0 : H * 2 * pairs, 0:C]


def whole_kernel(
    n,
    zone_ref, owner_hbm, feat_ref, mask_hbm, k_hbm, score_ref,
    owner_ref, mask_ref, tile, k_ref, w_ref, slots, stage, gold, zones,
    rows, pixels, t_ref, tb_ref, cross, res, stack, parts,
    gates, local, send1, recv1, send2, recv2, zsend, zrecv, part_send, part_recv,
):
    half = n // 2
    low_home, end_home = n // 4, n // 4 + half
    sub = W * C // FOLDS // half
    run = 8 * C
    me = lax.axis_index("col")
    block = me // BLOCK
    is_home = jnp.logical_and(me >= low_home, me < end_home)
    not_home = jnp.logical_not(is_home)
    mine = me - low_home

    tile_copy = pltpu.make_async_copy(feat_ref.at[0], tile, local.at[0])
    k_copy = pltpu.make_async_copy(k_hbm, k_ref, local.at[1])
    mask_copy = pltpu.make_async_copy(mask_hbm, mask_ref, local.at[2])
    owner_load = pltpu.make_async_copy(owner_hbm, owner_ref, local.at[3])
    tile_copy.start()

    def part_of(k, p):
        lane = p * sub
        at = lane // run * (FOLDS * run) + k * run + lax.rem(lane, run)
        return pl.ds(pl.multiple_of(at, PAIR), sub)

    def remote(src, dst, send_sem, recv_sem, dev):
        return pltpu.make_async_remote_copy(
            src_ref=src,
            dst_ref=dst,
            send_sem=send_sem,
            recv_sem=recv_sem,
            device_id={"col": dev},
            device_id_type=MESH,
        )

    def zone_copy(dev):
        return remote(zone_ref, zones.at[me], zsend, zrecv, dev)

    def spread(k, dev):
        piece = tile.at[:, part_of(k, dev - low_home)]
        return remote(piece, slots[k].at[me], send1.at[k], recv1.at[k], dev)

    def deliver(k, dev):
        return remote(stage[k].at[dev], gold[k].at[mine], send2.at[k], recv2.at[k], dev)

    def several(ref, count, send_sem, recv_sem):
        rest = ref.at[pl.ds(0, count)]
        return remote(rest, rest, send_sem, recv_sem, lax.rem(me + 1, n))

    def wait_homes(wait):
        @pl.when(is_home)
        def _():
            wait(half - 1)

        @pl.when(not_home)
        def _():
            wait(half)

    barrier = pltpu.get_barrier_semaphore()

    first_later = jnp.where(is_home, me + 1, jnp.maximum(me + 1, low_home))
    end_later = jnp.where(is_home, n, jnp.maximum(first_later, end_home))

    @pl.loop(first_later, end_later)
    def _(dev):
        pl.semaphore_signal(barrier, inc=1, device_id={"col": dev}, device_id_type=MESH)

    k_copy.start()
    mask_copy.start()
    owner_load.start()

    greetings = jnp.where(is_home, me, jnp.where(me < low_home, 0, half))

    @pl.when(greetings > 0)
    def _():
        pl.semaphore_wait(barrier, greetings)

    @pl.when(is_home)
    def _():
        @pl.loop(0, me)
        def _(dev):
            pl.semaphore_signal(gates.at[block], inc=1, device_id={"col": dev}, device_id_type=MESH)

    def send_zone(first, last):
        @pl.loop(first, last)
        def _(dev):
            zone_copy(dev).start()

    def send_to(k, first, last):
        @pl.loop(first, last)
        def _(dev):
            spread(k, dev).start()

    tile_copy.wait()
    earlier = jnp.clip(me, low_home, end_home)
    send_zone(low_home, earlier)
    for k in range(FOLDS):
        send_to(k, low_home, earlier)
    for b in range(low_home // BLOCK, end_home // BLOCK):
        first = jnp.maximum(me + 1, b * BLOCK)
        last = (b + 1) * BLOCK

        @pl.when(last > first)
        def _():
            pl.semaphore_wait(gates.at[b], last - first)
            send_zone(first, last)
            send_to(0, first, last)

    later = jnp.clip(me + 1, low_home, end_home)
    for k in range(1, FOLDS):
        send_to(k, later, end_home)
    lanes = [slice(t * PAIR, (t + 1) * PAIR) for t in range(W * C // PAIR)]
    t_f = to_pixels([tile[:, at] for at in lanes], rows, pixels).T
    t_ref[...] = t_f
    tb_ref[...] = t_f.astype(jnp.bfloat16)

    @pl.when(is_home)
    def _():
        for k in range(FOLDS):
            slots[k][me] = tile[:, part_of(k, mine)]

    k_copy.wait()
    for i in range(2):
        for dy in range(3):
            w_ref[i, dy * C : (dy + 1) * C, :] = k_ref[i, :, dy * 3 * C : (dy + 1) * 3 * C]
    mask_copy.wait()
    owner_load.wait()

    @pl.when(is_home)
    def _():
        several(zones, n - 1, zsend, zrecv).wait_recv()
        upper = me // half
        quarter = low_home
        flips = [*range(n - 1, half - 1, -1), *range(quarter)]
        wanted = [c + upper * (n - 1 - 2 * c) for c in flips]
        first_mate = quarter + upper * quarter
        at = me - first_mate
        wanted += [first_mate + lax.rem(at + o, quarter) for o in range(1, quarter)]
        wanted = [(dev, owner_ref[zones[dev, 0]]) for dev in wanted]
        for k in range(FOLDS):
            several(slots[k], n - 1, send1.at[k], recv1.at[k]).wait_recv()
            for dev, owner in wanted:
                stage[k][dev] = slots[k][owner]
                deliver(k, dev).start()
            gold[k][mine] = slots[k][owner_ref[zone_ref[0]]]

    row = lax.broadcasted_iota(jnp.int32, (8, W), 0)
    column = lax.broadcasted_iota(jnp.int32, (8, W), 1)

    def near(k, b):
        gap = 16 * b + 8 * k + row - column
        return jnp.logical_and(gap >= -8, gap < 8)

    def inside(k, b):
        gap = 16 * b + 8 * k + row - column
        return jnp.logical_and(gap >= -SHIFT, gap <= SHIFT)

    def fold(k, v):
        v = v.reshape(H, 8, 8, W)
        total = jnp.zeros((H, 8, W), jnp.float32)
        for b in range(8):
            total = jnp.where(near(k, b)[None], v[:, b], total)
        return total

    t_b = tb_ref[...]
    gts = []
    squares = []
    for k in range(FOLDS):
        wait_homes(lambda count: several(gold[k], count, send2.at[k], recv2.at[k]).wait_recv())
        places = [(p, at) for p in range(half) for at in range(0, sub, PAIR)]
        g_f = to_pixels([gold[k][p, :, at : at + PAIR] for p, at in places], rows, pixels)
        g = g_f.astype(jnp.bfloat16)
        gts.append(g_f.T.astype(jnp.bfloat16))
        for y in range(0, H, 2):
            gram = jnp.dot(g, t_b[:, y * W : (y + 2) * W], preferred_element_type=jnp.float32)
            for i in range(2):
                cross[y + i, :, 8 * k : 8 * k + 8, :] = fold(k, gram[:, i * W : (i + 1) * W])
        square = jnp.sum(g_f * g_f, axis=1, keepdims=True)
        squares.append(fold(k, jnp.broadcast_to(square, (H * W // FOLDS, W))))
    gt = jnp.concatenate(gts, axis=1)
    for y in range(H):
        cross[y] = diagonal_box(cross[y]) * SCALE
    other_rows = diagonal_box(jnp.concatenate(squares, axis=1))
    windows = {}

    def other_window(lo, hi):
        lo, hi = max(lo, 0), min(hi, H - 1)
        if (lo, hi) not in windows:
            total = other_rows[lo]
            for r in range(lo + 1, hi + 1):
                total = total + other_rows[r]
            windows[lo, hi] = total
        return windows[lo, hi]

    t_f = t_ref[...]
    own = jnp.sum(t_f * t_f, axis=0, keepdims=True)
    own_rows = [own[:, y * W : (y + 1) * W] for y in range(H)]
    slot = lax.broadcasted_iota(jnp.int32, (16, W), 0)
    shift = lax.rem(slot - lax.broadcasted_iota(jnp.int32, (16, W), 1) + W + 8, 16) - 8
    used = jnp.logical_and(shift >= -SHIFT, shift <= SHIFT)

    def weights_of(y):
        lo_y, hi_y = max(0, y - REACH), min(H - 1, y + REACH)
        self_energy = own_rows[lo_y]
        for r in range(lo_y + 1, hi_y + 1):
            self_energy = self_energy + own_rows[r]
        self_energy = jnp.broadcast_to(lane_box(self_energy), (16, W))
        denom = jnp.zeros((16, W), jnp.float32)
        picked = {}
        for a in range(-SHIFT, SHIFT + 1):
            num = None
            for r in range(lo_y, hi_y + 1):
                if 0 <= r + a < H:
                    num = cross[r, r + a] if num is None else num + cross[r, r + a]
            if num is None:
                denom = denom + 1.0
                continue
            expo = jnp.exp2(num * lax.rsqrt(self_energy * other_window(lo_y + a, hi_y + a) + 1e-05))
            if 0 <= y + a < H:
                picked[y + a] = expo.astype(jnp.bfloat16)
                expo = picked[y + a].astype(jnp.float32)
            denom = denom + expo
        total = jnp.sum(jnp.where(used, denom, 0.0), axis=0, keepdims=True)
        wides = []
        zeros = jnp.zeros((8, W), jnp.float32)
        for k in range(FOLDS):
            for r in range(H):
                value = picked[r].astype(jnp.float32)[8 * k : 8 * k + 8] if r in picked else zeros
                for b in range(8):
                    wides.append(jnp.where(inside(k, b), value, 0.0) if r in picked else zeros)
        return jnp.concatenate(wides, axis=0).astype(jnp.bfloat16), total

    for y in range(0, H, 2):
        pair = [weights_of(y), weights_of(y + 1)]
        wide = jnp.concatenate([p[0] for p in pair], axis=1)
        numer = jnp.dot(gt, wide, preferred_element_type=jnp.float32)
        total = jnp.concatenate([p[1] for p in pair], axis=1)
        cols = slice(y * W, (y + 2) * W)
        res[:, cols] = (t_f[:, cols] - numer / total).astype(jnp.bfloat16).astype(jnp.float32)

    residual = res[...]
    hidden = jnp.maximum(conv_rows(residual, stack, w_ref[0]), 0.0)
    hidden = hidden.astype(jnp.bfloat16).astype(jnp.float32)
    refined = residual + conv_rows(hidden, stack, w_ref[1])
    flat = jnp.sum(refined * refined, axis=0, keepdims=True) * (1.0 / C)
    energy = jnp.concatenate([flat[:, y * W : (y + 1) * W] for y in range(H)], axis=0)
    masked = mask_ref[0].astype(jnp.float32)
    die_sum = jnp.sum(jnp.sum(energy * masked, axis=1, keepdims=True), axis=0, keepdims=True)
    die_count = jnp.sum(jnp.sum(masked, axis=1, keepdims=True), axis=0, keepdims=True)
    lane = lax.broadcasted_iota(jnp.int32, (1, W), 1)
    zone = zone_ref[0]
    at_sum = lane == zone
    at_count = lane == zone + W // 2
    parts[me] = jnp.where(at_sum, die_sum, jnp.where(at_count, die_count, 0.0))

    def give(dev):
        return remote(parts.at[me], parts.at[me], part_send, part_recv, dev)

    upper = me // half
    for c in range(n - 1, half - 1, -1):
        give(c + upper * (n - 1 - 2 * c)).start()
    for o in range(1, half):
        give(upper * half + lax.rem(me + o, half)).start()

    wait_homes(lambda count: several(zones, count, zsend, zrecv).wait_send())
    for k in range(FOLDS):
        wait_homes(lambda count: several(slots[k], count, send1.at[k], recv1.at[k]).wait_send())

    @pl.when(is_home)
    def _():
        for k in range(FOLDS):
            several(stage[k], n - 1, send2.at[k], recv2.at[k]).wait_send()

    rest = parts.at[pl.ds(0, n - 1)]
    give_all = remote(rest, rest, part_send, part_recv, lax.rem(me + 1, n))
    give_all.wait_recv()
    total = jnp.sum(parts[...], axis=0)
    zone_sum = jnp.sum(jnp.where(at_sum, total, 0.0), axis=1, keepdims=True)
    zone_count = jnp.sum(jnp.where(at_count, total, 0.0), axis=1, keepdims=True)
    mean = zone_sum / jnp.maximum(zone_count, 1.0)
    score_ref[0] = energy / (mean + 0.01)
    give_all.wait_send()


def body(n, features, zone_ids, golden_owner, defect_mask, kernels):
    half = n // 2
    sub = W * C // FOLDS // half
    vmem = pl.BlockSpec(memory_space=pltpu.VMEM)
    hbm = pl.BlockSpec(memory_space=pl.ANY)
    dma = pltpu.SemaphoreType.DMA
    return pl.pallas_call(
        functools.partial(whole_kernel, n),
        out_shape=jax.ShapeDtypeStruct((1, H, W), jnp.float32),
        in_specs=[pl.BlockSpec(memory_space=pltpu.SMEM), hbm, hbm, hbm, hbm],
        out_specs=vmem,
        scratch_shapes=[
            pltpu.SMEM(golden_owner.shape, jnp.int32),
            pltpu.VMEM((1, H, W), jnp.int32),
            pltpu.VMEM((H, W * C), jnp.bfloat16),
            pltpu.VMEM((2, C, 9 * C), jnp.bfloat16),
            pltpu.VMEM((2, 3 * C, 3 * C), jnp.bfloat16),
            [pltpu.VMEM((n, H, sub), jnp.bfloat16)] * FOLDS,
            [pltpu.VMEM((n, H, sub), jnp.bfloat16)] * FOLDS,
            [pltpu.VMEM((half, H, sub), jnp.bfloat16)] * FOLDS,
            pltpu.SMEM((n, 1), jnp.int32),
            pltpu.VMEM((H * W * C // 128, 128), jnp.float32),
            pltpu.VMEM((H * W, 128), jnp.float32),
            pltpu.VMEM((C, H * W), jnp.float32),
            pltpu.VMEM((C, H * W), jnp.bfloat16),
            pltpu.VMEM((H, H, 16, W), jnp.float32),
            pltpu.VMEM((C, H * W), jnp.float32),
            pltpu.VMEM((3 * C, H * W), jnp.bfloat16),
            pltpu.VMEM((n, 1, W), jnp.float32),
            pltpu.SemaphoreType.REGULAR((n // BLOCK,)),
            dma((4,)),
            dma((FOLDS,)),
            dma((FOLDS,)),
            dma((FOLDS,)),
            dma((FOLDS,)),
            dma,
            dma,
            dma,
            dma,
        ],
        compiler_params=pltpu.CompilerParams(collective_id=0, has_side_effects=True, vmem_limit_bytes=24 * 1024 * 1024
        ),
    )(zone_ids, *[pltpu.with_memory_space_constraint(v, pltpu.HBM) for v in (golden_owner, features, defect_mask, jnp.swapaxes(kernels, 1, 2))])


def solution(mesh):
    in_specs = (
        P(("groups", "col"), None, None),
        P(("groups", "col")),
        P("groups"),
        P(("groups", "col"), None, None),
        P(),
    )
    out_specs = P(("groups", "col"), None, None)
    run = functools.partial(body, mesh.shape["col"])
    return jax.shard_map(run, mesh=mesh, in_specs=in_specs, out_specs=out_specs, check_vma=False)
```
